128 devices in a mesh: traj: 4 (over y_lo, core), tx: 8 (over y_hi, z), ty: 4 (over x).
Axes of the slice: x: 4, y: 4 (y_hi: 2, y_lo: 2; y = y_hi * 2 + y_lo), z: 4, core: 2. Of those that a mesh axis runs over, the one named last changes fastest.
Arguments:
- density: float32 [4, 256, 4096], P('traj', None, ('tx', 'ty')), may hold values from 1 to 2
- momentum: float32 [4, 2, 256, 4096], P('traj', None, None, ('tx', 'ty')), may hold values from -0.5 to 0.5
- tracer: float32 [4, 256, 4096], P('traj', None, ('tx', 'ty')), may hold values from -1 to 1
- cotangent: float32 [4, 4, 256, 4096], P('traj', None, None, ('tx', 'ty')), may hold values from -6 to 6
- w_in: float32 [32, 16], replicated, may hold values from -1.5 to 1.5
- b_in: float32 [32], replicated, may hold values from -3 to 3
- w_mid: float32 [32, 32], replicated, may hold values from -1 to 1
- b_mid: float32 [32], replicated, may hold values from -3 to 3
- w_out: float32 [8, 32], replicated, may hold values from -1 to 1
- b_out: float32 [8], replicated, may hold values from -3 to 3
Outputs:
- grad_density: float32 [4, 256, 4096], P('traj', None, ('tx', 'ty'))
- grad_momentum: float32 [4, 2, 256, 4096], P('traj', None, None, ('tx', 'ty'))
- grad_tracer: float32 [4, 256, 4096], P('traj', None, ('tx', 'ty'))
- grad_w_in: float32 [32, 16], replicated
- grad_b_in: float32 [32], replicated
- grad_w_mid: float32 [32, 32], replicated
- grad_b_mid: float32 [32], replicated
- grad_w_out: float32 [8, 32], replicated
- grad_b_out: float32 [8], replicated
The draws below stay inside these ranges and needn't reach their ends.
All inputs are finite; a program needn't handle non-finite values.
Results may differ from the reference program's by a relative error of at most 0.0003.
Values sent between devices are 32-bit elements; how exact they have to be, the bound alone decides.
A program may use at most 128 MiB of HBM per device.

```python
import jax
import jax.numpy as jnp
from jax import lax

NX = 256
HID = 32
TRAJ = 4
NY = 4096


def steps_of(rng, extent, cuts, low, top_value):
    level, own = 1.0, jax.random.fold_in(rng, 6)
    for axis_at, shards_of in cuts:
        draws = jnp.exp(jax.random.uniform(jax.random.fold_in(own, axis_at), (shards_of,), jnp.float32, low / len(cuts), top_value / len(cuts)))
        level = level * jnp.repeat(draws, extent[axis_at] // shards_of).reshape([-1 if axis == axis_at else 1 for axis in range(len(extent))])
    return level


def scatter_about(stream_key, shape, spread, bound, cuts=(), dtype=jnp.bfloat16):
    level = steps_of(stream_key, shape, cuts, -0.22, 0.18) if cuts else 1.0
    entries = jax.random.normal(stream_key, shape, jnp.float32) * spread * level
    return jnp.minimum(jnp.maximum(entries, -bound), bound).astype(dtype)


def setup_inputs(seed: int = 0) -> dict:
    arg_keys = jax.random.split(jax.random.key(seed), 11)
    density = jnp.clip(1.0 + 1.0 * jax.random.uniform(arg_keys[0], (TRAJ, NX, NY), jnp.float32) ** steps_of(arg_keys[0], (TRAJ, NX, NY), ((0, 4), (2, 32)), -0.2, 0.2), 1.0, 2.0)
    momentum = jnp.clip(jax.random.uniform(arg_keys[1], (TRAJ, 2, NX, NY), jnp.float32, -0.5, 0.5) * steps_of(arg_keys[1], (TRAJ, 2, NX, NY), ((0, 4), (3, 32)), -0.4, 0.0), -0.5, 0.5)
    tracer = jnp.clip(jax.random.uniform(arg_keys[2], (TRAJ, NX, NY), jnp.float32, -1.0, 1.0) * steps_of(arg_keys[2], (TRAJ, NX, NY), ((0, 4), (2, 32)), -0.4, 0.0), -1.0, 1.0)
    cotangent = scatter_about(arg_keys[3], (TRAJ, 4, NX, NY), 1.0, 6.0, ((0, 4), (3, 32)), jnp.float32)
    w_in = scatter_about(arg_keys[4], (HID, 16), 16 ** -0.5, 1.5, (), jnp.float32)
    b_in = scatter_about(arg_keys[5], (HID,), 0.5, 3.0, (), jnp.float32)
    w_mid = scatter_about(arg_keys[6], (HID, HID), HID ** -0.5, 1.0, (), jnp.float32)
    b_mid = scatter_about(arg_keys[7], (HID,), 0.5, 3.0, (), jnp.float32)
    w_out = scatter_about(arg_keys[8], (8, HID), HID ** -0.5, 1.0, (), jnp.float32)
    b_out = scatter_about(arg_keys[9], (8,), 0.5, 3.0, (), jnp.float32)
    return {"density": density, "momentum": momentum, "tracer": tracer, "cotangent": cotangent, "w_in": w_in, "b_in": b_in, "w_mid": w_mid, "b_mid": b_mid, "w_out": w_out, "b_out": b_out}


courant = 0.1
slope_gain = 0.25

def take_cells(values, sweep_dim, first_index, cell_count):
    return lax.slice_in_dim(values, first_index, first_index + cell_count, axis=sweep_dim)

def wrap_pad(values, sweep_dim, rim_width):
    total = values.shape[sweep_dim]
    return jnp.concatenate([take_cells(values, sweep_dim, total - rim_width, rim_width), values, take_cells(values, sweep_dim, 0, rim_width)], sweep_dim)

def expand(vector):
    return vector.reshape(vector.shape + (1, 1))

def limiter(window, weights):
    w_in, b_in, w_mid, b_mid, w_out, b_out = weights
    highest = lax.Precision.HIGHEST
    hidden_first = jnp.tanh(jnp.einsum('hc,cxy->hxy', w_in, window, precision=highest) + expand(b_in))
    hidden_second = jnp.tanh(jnp.einsum('hc,cxy->hxy', w_mid, hidden_first, precision=highest) + expand(b_mid))
    return jnp.tanh(jnp.einsum('hc,cxy->hxy', w_out, hidden_second, precision=highest) + expand(b_out))

def physical_flux(states, velocity):
    return jnp.stack([states[1], states[1] * velocity + states[0], states[2] * velocity, states[3] * velocity])

def face_flux(left_state, right_state):
    velocity_left = left_state[1] / left_state[0]
    velocity_right = right_state[1] / right_state[0]
    wave_speed = jnp.maximum(jnp.abs(velocity_left), jnp.abs(velocity_right)) + 1.0
    mean_flux = 0.5 * (physical_flux(left_state, velocity_left) + physical_flux(right_state, velocity_right))
    return mean_flux - 0.5 * wave_speed * (right_state - left_state)

def swap_momenta(values):
    return jnp.stack([values[0], values[2], values[1], values[3]])

def sweep(padded, sweep_dim, rotate, weights):
    if rotate:
        padded = swap_momenta(padded)
    length = padded.shape[sweep_dim] - 4
    face_count = length + 1
    shifted = [take_cells(padded, sweep_dim, offset, face_count) for offset in range(4)]
    window = jnp.concatenate(shifted, 0)
    gate_values = limiter(window, weights)
    left_state = shifted[1] + slope_gain * gate_values[:4] * (shifted[2] - shifted[0])
    right_state = shifted[2] - slope_gain * gate_values[4:] * (shifted[3] - shifted[1])
    fluxes = face_flux(left_state, right_state)
    cell_values = take_cells(padded, sweep_dim, 2, length)
    updated = cell_values - courant * (take_cells(fluxes, sweep_dim, 1, length) - take_cells(fluxes, sweep_dim, 0, length))
    if rotate:
        updated = swap_momenta(updated)
    return updated

def forward(states, weights):
    middle = sweep(wrap_pad(states, 1, 2), 1, False, weights)
    return sweep(wrap_pad(middle, 2, 2), 2, True, weights)

def reference(density, momentum, tracer, cotangent, w_in, b_in, w_mid, b_mid, w_out, b_out):
    weights = (w_in, b_in, w_mid, b_mid, w_out, b_out)
    states = jnp.concatenate([density[:, None], momentum, tracer[:, None]], 1)

    def single_flow(flow_pair):
        flow_state, flow_cot = flow_pair
        _, pull_back = jax.vjp(forward, flow_state, weights)
        return pull_back(flow_cot)
    grad_state, grad_weights = lax.map(single_flow, (states, cotangent))
    grad_weights = jax.tree.map(lambda stacked: lax.optimization_barrier(jnp.sum(stacked, 0)), grad_weights)
    return (grad_state[:, 0], grad_state[:, 1:3], grad_state[:, 3], grad_weights[0], grad_weights[1], grad_weights[2], grad_weights[3], grad_weights[4], grad_weights[5])
```

```python
import jax
import jax.numpy as jnp
from jax import lax
from jax.experimental import pallas as pl
from jax.experimental.pallas import tpu as pltpu
from jax.sharding import PartitionSpec as P

F32 = jnp.float32
BF16 = jnp.bfloat16
courant = 0.1
slope_gain = 0.25
HALO = 4
RING = ("tx", "ty")
Y_ORDER = (0, 2, 1, 3)


def split(x):
    hi = x.astype(BF16)
    return hi, (x - hi.astype(F32)).astype(BF16)


def split3(x):
    hi = x.astype(BF16)
    rest = x - hi.astype(F32)
    mid = rest.astype(BF16)
    return hi, mid, (rest - mid.astype(F32)).astype(BF16)


def six(parts, ones):
    hi, mid, low = parts
    return rows(hi, mid, low, hi, mid, hi, ones)


def dot(a, b):
    return lax.dot_general(a, b, (((1,), (0,)), ((), ())), preferred_element_type=F32)


def dot_nt(a, b):
    return lax.dot_general(a, b, (((1,), (1,)), ((), ())), preferred_element_type=F32)


def exact(a, b, nt=False):
    dims = (((1,), (1 if nt else 0,)), ((), ()))
    return lax.dot_general(a, b, dims, preferred_element_type=F32, precision=lax.Precision.HIGHEST)


def rows(*parts):
    return jnp.concatenate(parts, 0)


def lanes(*parts):
    return jnp.concatenate(parts, 1)


def roll(v, amount):
    return pltpu.roll(v, amount % v.shape[1], 1)


def halves_at(lead, at):
    return [tuple(lead) + (t, at, slice(None)) for t in range(2)]


def get(ref, lead, at):
    return lanes(*[ref[where] for where in halves_at(lead, at)])


def put(ref, lead, at, value):
    for t, where in enumerate(halves_at(lead, at)):
        ref[where] = value[:, 128 * t : 128 * t + 128]


def face_states(cells, gates):
    below, here, above, above2 = cells
    slope_left = [above[c] - below[c] for c in range(4)]
    slope_right = [above2[c] - here[c] for c in range(4)]
    left = [here[c] + slope_gain * gates[c] * slope_left[c] for c in range(4)]
    right = [above[c] - slope_gain * gates[4 + c] * slope_right[c] for c in range(4)]
    return slope_left, slope_right, left, right


def flux_of(left, right):
    u_left = left[1] * (1.0 / left[0])
    u_right = right[1] * (1.0 / right[0])
    speed = 0.5 * jnp.maximum(jnp.abs(u_left), jnp.abs(u_right)) + 0.5
    physical = (
        left[1] + right[1],
        left[1] * u_left + left[0] + (right[1] * u_right + right[0]),
        left[2] * u_left + right[2] * u_right,
        left[3] * u_left + right[3] * u_right,
    )
    return [0.5 * physical[c] - speed * (right[c] - left[c]) for c in range(4)]


def flux_back(cells, gates, cot):
    slope_left, slope_right, left, right = face_states(cells, gates)
    inv_left = 1.0 / left[0]
    inv_right = 1.0 / right[0]
    u_left = left[1] * inv_left
    u_right = right[1] * inv_right
    abs_left = jnp.abs(u_left)
    abs_right = jnp.abs(u_right)
    half = [0.5 * v for v in cot]
    speed = jnp.maximum(abs_left, abs_right) + 1.0
    d_speed = half[0] * (left[0] - right[0])
    for c in range(1, 4):
        d_speed = d_speed + half[c] * (left[c] - right[c])
    share_left = jnp.where(abs_left > abs_right, 1.0, jnp.where(abs_left < abs_right, 0.0, 0.5))
    d_abs_left = d_speed * share_left
    d_abs_right = d_speed - d_abs_left

    def one_side(state, inv, u, d_abs, sign):
        signed = jnp.where(u > 0.0, d_abs, jnp.where(u < 0.0, -d_abs, 0.0))
        d_u = half[1] * state[1] + half[2] * state[2] + half[3] * state[3] + signed
        d_u = d_u * inv
        visc = [sign * (speed * half[c]) for c in range(4)]
        return (
            half[1] - d_u * u + visc[0],
            half[0] + half[1] * u + d_u + visc[1],
            half[2] * u + visc[2],
            half[3] * u + visc[3],
        )

    d_left = one_side(left, inv_left, u_left, d_abs_left, 1.0)
    d_right = one_side(right, inv_right, u_right, d_abs_right, -1.0)
    scaled_left = [slope_gain * v for v in d_left]
    scaled_right = [slope_gain * v for v in d_right]
    d_gates = [scaled_left[c] * slope_left[c] for c in range(4)]
    d_gates += [-(scaled_right[c] * slope_right[c]) for c in range(4)]
    minus_below = [gates[c] * scaled_left[c] for c in range(4)]
    minus_above2 = [gates[4 + c] * scaled_right[c] for c in range(4)]
    to_here = [d_left[c] + minus_above2[c] for c in range(4)]
    to_above = [d_right[c] + minus_below[c] for c in range(4)]
    return d_gates, minus_below, to_here, to_above, minus_above2


def kernel(
    density, momentum, tracer, cotangent, halo,
    w_x, w_y, w_m, w_o, w_ot, w_mt, w_xt, w_yt,
    g_density, g_momentum, g_tracer, packed,
    nat, cot, mid, mid_hi, mid_lo, mid_lo2,
    h1_hi, h1_lo, h2_hi, h2_lo, t_hi, t_lo, gate_x,
    face, d_mix, out_nat,
    xi, gi, di, mi, zi,
    acc_x, acc_y, acc_m, acc_o,
):
    width = nat.shape[2]
    own = density.shape[2]
    blocks = own // 8
    ones = jnp.ones((16, width), BF16)

    for c in range(4):
        if c == 0:
            source = density[0]
        elif c == 3:
            source = tracer[0]
        else:
            source = momentum[0, c - 1]
        nat[c, 8 : 8 + own, :] = source.T
        nat[c, 0:8, :] = halo[c]
        put(cot, (c,), pl.ds(8, own), cotangent[0, c].T)
        put(cot, (c,), pl.ds(0, 8), halo[4 + c])
        put(cot, (c,), pl.ds(8 + own, 8), halo[4 + c])
    acc_x[...] = jnp.zeros_like(acc_x)
    acc_y[...] = jnp.zeros_like(acc_y)
    acc_m[...] = jnp.zeros_like(acc_m)
    acc_o[...] = jnp.zeros_like(acc_o)

    def upper_layers(first):
        first_parts = split3(first)
        seconds, gate_rows = [], []
        for line in range(4):
            at = slice(32 * line, 32 * line + 32)
            operand = six([part[at] for part in first_parts], ones)
            second = split3(jnp.tanh(dot(w_m[...], operand)))
            seconds.append(second)
            gate_rows.append(jnp.tanh(dot(w_o[...], six(second, ones))))
        return (
            first_parts[0],
            first_parts[1],
            rows(*[v[0] for v in seconds]),
            rows(*[v[1] for v in seconds]),
            rows(*gate_rows),
        )

    def limiter_back(gates, d_gates, load_first, load_second):
        for g in range(8):
            put(di, (), pl.ds(g, 8, stride=8), d_gates[g] * (1.0 - gates[g] * gates[g]))
        d_first, mid_lhs, mid_rhs, out_lhs, out_rhs = [], [], [], [], []
        for pair in range(4):
            o_hi, o_lo = split(get(di, (), pl.ds(16 * pair, 16)))
            s_hi, s_lo = load_second(pair)
            f_hi, f_lo = load_first(pair)
            second = s_hi.astype(F32) + s_lo.astype(F32)
            d_second = dot(w_ot[...], rows(o_hi, o_lo, o_hi)) * (1.0 - second * second)
            m_hi, m_lo = split(d_second)
            first = f_hi.astype(F32) + f_lo.astype(F32)
            d_one = dot(w_mt[...], rows(m_hi, m_lo, m_hi)) * (1.0 - first * first)
            d_first.append(split(d_one))
            for line in range(2):
                at = slice(32 * line, 32 * line + 32)
                mid_lhs.append(rows(m_hi[at], m_lo[at]))
                mid_rhs.append(rows(f_hi[at], f_lo[at], ones))
            out_lhs.append(rows(o_hi, o_lo))
            out_rhs.append(rows(s_hi, s_lo, ones))
        acc_m[...] += dot_nt(lanes(*mid_lhs), lanes(*mid_rhs))
        acc_o[...] += dot_nt(lanes(*out_lhs), lanes(*out_rhs))
        return d_first

    def x_forward(b, carry):
        n0 = pl.multiple_of(8 * b, 8)
        here = [nat[c, pl.ds(n0, 8), :] for c in range(4)]
        cells = [[roll(v, 1) for v in here], here, [roll(v, -1) for v in here], [roll(v, -2) for v in here]]
        for s in range(4):
            for c in range(4):
                put(xi, (), pl.ds(4 * s + c, 8, stride=16), cells[s][c])
        for q in range(2):
            window = split3(get(xi, (), pl.ds(64 * q, 64)))
            at = pl.ds(pl.multiple_of(128 * b + 64 * q, 64), 64)
            t_hi[at, :] = window[0]
            t_lo[at, :] = window[1]
            firsts = []
            for line in range(4):
                at = slice(16 * line, 16 * line + 16)
                firsts.append(dot(w_x[...], six([part[at] for part in window], ones)))
            first = jnp.tanh(rows(*firsts))
            f_hi, f_lo, s_hi, s_lo, gate_rows = upper_layers(first)
            at = pl.ds(pl.multiple_of(256 * b + 128 * q, 128), 128)
            h1_hi[at, :] = f_hi
            h1_lo[at, :] = f_lo
            h2_hi[at, :] = s_hi
            h2_lo[at, :] = s_lo
            put(gi, (), pl.ds(32 * q, 32), gate_rows)
        gates = [get(gi, (), pl.ds(g, 8, stride=8)) for g in range(8)]
        for g in range(8):
            gate_x[g, pl.ds(n0, 8), :] = gates[g]
        _, _, left, right = face_states(cells, gates)
        fluxes = flux_of(left, right)
        for c in range(4):
            value = here[c] - courant * (fluxes[c] - roll(fluxes[c], 1))
            put(mid, (c,), pl.ds(n0, 8), value)
            put(mi, (), pl.ds(Y_ORDER[c], 8, stride=4), value)
        at = pl.ds(pl.multiple_of(32 * b, 32), 32)
        for ref, part in zip((mid_hi, mid_lo, mid_lo2), split3(get(mi, (), pl.ds(0, 32)))):
            ref[at, :] = part
        return carry

    lax.fori_loop(0, blocks + 1, x_forward, 0)
    mid[:, :, 8 + own : 16 + own, :] = mid[:, :, 0:8, :]
    for ref in (mid_hi, mid_lo, mid_lo2):
        ref[4 * own + 32 : 4 * own + 64, :] = ref[0:32, :]
    d_mix[:, 0:16, :] = jnp.zeros((2, 16, 128), F32)

    def y_sweep(b, carry):
        n0 = pl.multiple_of(8 * b, 8)
        saved, windows = [], []
        for q in range(2):
            at = pl.ds(pl.multiple_of(32 * b + 16 * q, 16), 32)
            window = mid_hi[at, :], mid_lo[at, :], mid_lo2[at, :]
            windows.append(rows(window[0], window[1], ones))
            first = jnp.tanh(dot(w_y[...], six(window, ones)))
            parts = upper_layers(first)
            saved.append(parts)
            put(gi, (), pl.ds(32 * q, 32), parts[4])
        gates = [get(gi, (), pl.ds(g, 8, stride=8)) for g in range(8)]
        cells = [[get(mid, (c,), pl.ds(n0 + k, 8)) for c in Y_ORDER] for k in range(4)]
        cots = [courant * (get(cot, (c,), pl.ds(n0 + 2, 8)) - get(cot, (c,), pl.ds(n0 + 1, 8))) for c in Y_ORDER]
        d_gates, minus_below, to_here, to_above, minus_above2 = flux_back(cells, gates, cots)
        for c in range(4):
            to = Y_ORDER[c]
            put(face, (to,), pl.ds(n0, 8), minus_below[c])
            put(face, (4 + to,), pl.ds(n0, 8), to_here[c])
            put(face, (8 + to,), pl.ds(n0, 8), to_above[c])
            put(face, (12 + to,), pl.ds(n0, 8), minus_above2[c])

        def load(part):
            def of(pair):
                at = slice(64 * (pair % 2), 64 * (pair % 2) + 64)
                return saved[pair // 2][part][at], saved[pair // 2][part + 1][at]
            return of

        d_first = limiter_back(gates, d_gates, load(0), load(2))
        outs, right_side = [], []
        for q in range(2):
            hi = rows(d_first[2 * q][0], d_first[2 * q + 1][0])
            lo = rows(d_first[2 * q][1], d_first[2 * q + 1][1])
            outs.append(dot(w_yt[...], rows(hi, lo, hi)))
            right_side.append(rows(hi, lo))
        at = pl.multiple_of(32 * b, 32)
        put(d_mix, (), pl.ds(at, 16), get(d_mix, (), pl.ds(at, 16)) + outs[0][:16])
        put(d_mix, (), pl.ds(at + 16, 16), outs[0][16:] + outs[1][:16])
        put(d_mix, (), pl.ds(at + 32, 16), outs[1][16:])
        acc_y[...] += dot_nt(lanes(*windows), lanes(*right_side))

        @pl.when(b == 0)
        def _():
            acc_y[...] = jnp.zeros_like(acc_y)
            acc_m[...] = jnp.zeros_like(acc_m)
            acc_o[...] = jnp.zeros_like(acc_o)

        return carry

    lax.fori_loop(0, blocks + 1, y_sweep, 0)

    def x_back(b, carry):
        n0 = pl.multiple_of(8 * b, 8)
        gates = [gate_x[g, pl.ds(n0, 8), :] for g in range(8)]
        here = [nat[c, pl.ds(n0, 8), :] for c in range(4)]
        cells = [[roll(v, 1) for v in here], here, [roll(v, -1) for v in here], [roll(v, -2) for v in here]]
        back = []
        for c in range(4):
            value = get(cot, (c,), pl.ds(n0, 8)) + get(d_mix, (), pl.ds(4 * n0 + Y_ORDER[c], 8, stride=4))
            value = value + get(face, (4 + c,), pl.ds(n0 - 1, 8)) - get(face, (c,), pl.ds(n0, 8))
            value = value + get(face, (8 + c,), pl.ds(n0 - 2, 8)) - get(face, (12 + c,), pl.ds(n0 - 3, 8))
            back.append(value)
        cots = [courant * (roll(v, -1) - v) for v in back]
        d_gates, minus_below, to_here, to_above, minus_above2 = flux_back(cells, gates, cots)

        def load(hi_ref, lo_ref):
            def of(pair):
                at = pl.ds(pl.multiple_of(256 * b + 64 * pair, 64), 64)
                return hi_ref[at, :], lo_ref[at, :]
            return of

        d_first = limiter_back(gates, d_gates, load(h1_hi, h1_lo), load(h2_hi, h2_lo))
        left_side, right_side = [], []
        for line in range(8):
            at = pl.ds(pl.multiple_of(128 * b + 16 * line, 16), 16)
            left_side.append(rows(t_hi[at, :], t_lo[at, :], ones))
            at = slice(32 * (line % 2), 32 * (line % 2) + 32)
            hi, lo = [v[at] for v in d_first[line // 2]]
            right_side.append(rows(hi, lo))
            put(zi, (), pl.ds(16 * line, 16), dot(w_xt[...], rows(hi, lo, hi)))
        acc_x[...] += dot_nt(lanes(*left_side), lanes(*right_side))
        for c in range(4):
            parts = [get(zi, (), pl.ds(4 * s + c, 8, stride=16)) for s in range(4)]
            value = back[c] + to_here[c] + parts[1] + roll(parts[0] - minus_below[c], -1)
            value = value + roll(to_above[c] + parts[2], 1) + roll(parts[3] - minus_above2[c], 2)
            out_nat[c, pl.ds(pl.multiple_of(n0 - 8, 8), 8), :] = value
        return carry

    lax.fori_loop(1, blocks + 1, x_back, 0)

    g_density[0] = out_nat[0].T
    g_momentum[0, 0] = out_nat[1].T
    g_momentum[0, 1] = out_nat[2].T
    g_tracer[0] = out_nat[3].T

    def index(shape, axis):
        return lax.broadcasted_iota(jnp.int32, shape, axis)

    def indicator(condition):
        return jnp.where(condition, 1.0, 0.0).astype(F32)

    r, k = index((24, 48), 0), index((24, 48), 1)
    pick = jnp.where(k < 32, k % 16, jnp.where(k == 32, 16, -1))
    first = exact(indicator(r == pick), acc_x[...])
    r, k = index((32, 64), 0), index((32, 64), 1)
    by_unit = exact(indicator(r == k % 32), first, nt=True)
    first = jnp.zeros((24, 256), F32)
    r, k = index((80, 256), 0), index((80, 256), 1)
    distance = (r // 4) % 8 - (k // 32) % 4
    for s in range(4):
        masked = jnp.where(jnp.logical_and(r < 64, distance == s), acc_y[...], 0.0)
        rr, kk = index((24, 80), 0), index((24, 80), 1)
        first = first + exact(indicator(jnp.logical_and(rr == 4 * s + kk % 4, kk < 64)), masked)
    masked = jnp.where(r == 64, acc_y[...], 0.0)
    rr, kk = index((24, 80), 0), index((24, 80), 1)
    first = first + exact(indicator(jnp.logical_and(rr == 16, kk == 64)), masked)
    r, k = index((32, 256), 0), index((32, 256), 1)
    by_unit = by_unit + exact(indicator(r == k % 32), first, nt=True)
    r, k = index((24, 128), 0), index((24, 128), 1)
    total = exact(by_unit, indicator(jnp.logical_and(k == r + 64, r <= 16)))
    r, k = index((32, 64), 0), index((32, 64), 1)
    summed = exact(indicator(r == k % 32), acc_m[...])
    r, k = index((80, 128), 0), index((80, 128), 1)
    place = jnp.where(r < 64, r % 32, jnp.where(r == 64, 32, -1))
    total = total + exact(summed, indicator(k == place))
    r, k = index((32, 144), 0), index((32, 144), 1)
    same = jnp.logical_or(k >= 128, (r // 8) % 2 == (k // 32) % 2)
    masked = jnp.where(same, acc_o[...], 0.0)
    r, k = index((8, 32), 0), index((8, 32), 1)
    summed = exact(indicator(r == k % 8), masked)
    r, k = index((144, 128), 0), index((144, 128), 1)
    place = jnp.where(r < 128, r % 32, jnp.where(r == 128, 32, -1))
    packed[0:32, :] = total
    packed[32:40, :] = exact(summed, indicator(k == place))


def weight_blocks(w_in, b_in, w_mid, b_mid, w_out, b_out):
    def parts_of(v):
        hi = lax.reduce_precision(v, 8, 7)
        mid = lax.reduce_precision(v - hi, 8, 7)
        return hi, mid, lax.reduce_precision(v - hi - mid, 8, 7)

    def triple(grow, v):
        hi, mid, _ = parts_of(v)
        return jnp.concatenate([grow(hi), grow(hi), grow(mid)], 1)

    def sixfold(grow, v, bias, count):
        hi, mid, low = parts_of(v)
        columns = jnp.stack([jnp.tile(part, count) for part in parts_of(bias)], 1)
        columns = jnp.pad(columns, ((0, 0), (0, 13)))
        hi, mid, low = grow(hi), grow(mid), grow(low)
        return jnp.concatenate([hi, hi, hi, mid, mid, low, columns], 1)

    def grow_y(v):
        shifts = v.reshape(32, 4, 4)
        lines = [jnp.pad(shifts, ((0, 0), (k, 4 - k), (0, 0))) for k in range(4)]
        return jnp.stack(lines, 0).reshape(128, 32)

    def grow_pair(v):
        eye = jnp.eye(2, dtype=F32)
        return (eye[:, None, :, None] * v[None, :, None, :]).reshape(2 * v.shape[0], 2 * v.shape[1])

    def same(v):
        return v

    w_x = sixfold(same, w_in, b_in, 1)
    w_y = sixfold(grow_y, w_in, b_in, 4)
    w_m = sixfold(same, w_mid, b_mid, 1)
    w_o = sixfold(same, w_out, b_out, 1)
    w_ot = triple(grow_pair, w_out.T)
    w_mt = triple(grow_pair, w_mid.T)
    w_xt = triple(same, w_in.T)
    w_yt = triple(lambda v: grow_y(v).T, w_in)
    return [v.astype(BF16) for v in (w_x, w_y, w_m, w_o, w_ot, w_mt, w_xt, w_yt)]


def ring_size(mesh):
    return mesh.shape["tx"] * mesh.shape["ty"]


def make_body(size):
    def body(density, momentum, tracer, cotangent, w_in, b_in, w_mid, b_mid, w_out, b_out):
        own, width = density.shape[2], density.shape[1]
        states = jnp.concatenate([density[:, None], momentum, tracer[:, None], cotangent], 1)[0]
        low = jnp.swapaxes(states[:, :, :HALO], 1, 2)
        high = jnp.swapaxes(states[:, :, own - HALO :], 1, 2)
        from_right = lax.ppermute(low, RING, [((i + 1) % size, i) for i in range(size)])
        from_left = lax.ppermute(high, RING, [(i, (i + 1) % size) for i in range(size)])
        halo = jnp.concatenate([from_right, from_left], 1)
        weights = weight_blocks(w_in, b_in, w_mid, b_mid, w_out, b_out)
        extra = own + 16
        lines = own + 8
        out = pl.pallas_call(
            kernel,
            out_shape=(
                jax.ShapeDtypeStruct(density.shape, F32),
                jax.ShapeDtypeStruct(momentum.shape, F32),
                jax.ShapeDtypeStruct(tracer.shape, F32),
                jax.ShapeDtypeStruct((40, 128), F32),
            ),
            in_specs=[pl.BlockSpec(memory_space=pltpu.VMEM)] * 13,
            out_specs=tuple([pl.BlockSpec(memory_space=pltpu.VMEM)] * 4),
            scratch_shapes=[
                pltpu.VMEM((4, lines, width), F32),
                pltpu.VMEM((4, 2, extra, 128), F32),
                pltpu.VMEM((4, 2, extra, 128), F32),
                pltpu.VMEM((4 * extra, width), BF16),
                pltpu.VMEM((4 * extra, width), BF16),
                pltpu.VMEM((4 * extra, width), BF16),
                pltpu.VMEM((32 * lines, width), BF16),
                pltpu.VMEM((32 * lines, width), BF16),
                pltpu.VMEM((32 * lines, width), BF16),
                pltpu.VMEM((32 * lines, width), BF16),
                pltpu.VMEM((16 * lines, width), BF16),
                pltpu.VMEM((16 * lines, width), BF16),
                pltpu.VMEM((8, lines, width), F32),
                pltpu.VMEM((16, 2, extra, 128), F32),
                pltpu.VMEM((2, 4 * extra, 128), F32),
                pltpu.VMEM((4, own, width), F32),
                pltpu.VMEM((2, 128, 128), F32),
                pltpu.VMEM((2, 64, 128), F32),
                pltpu.VMEM((2, 64, 128), F32),
                pltpu.VMEM((2, 32, 128), F32),
                pltpu.VMEM((2, 128, 128), F32),
                pltpu.VMEM((48, 64), F32),
                pltpu.VMEM((80, 256), F32),
                pltpu.VMEM((64, 80), F32),
                pltpu.VMEM((32, 144), F32),
            ],
            compiler_params=pltpu.CompilerParams(vmem_limit_bytes=60 * 1024 * 1024),
        )(density, momentum, tracer, cotangent, halo, *weights)
        total = lax.psum(out[3], ("traj", "tx", "ty"))
        return (
            out[0],
            out[1],
            out[2],
            total[0:32, 64:80],
            total[0:32, 80],
            total[0:32, 0:32],
            total[0:32, 32],
            total[32:40, 0:32],
            total[32:40, 32],
        )

    return body


def solution(mesh):
    in_specs = (
        P("traj", None, ("tx", "ty")),
        P("traj", None, None, ("tx", "ty")),
        P("traj", None, ("tx", "ty")),
        P("traj", None, None, ("tx", "ty")),
        P(), P(), P(), P(), P(), P(),
    )
    out_specs = (
        P("traj", None, ("tx", "ty")),
        P("traj", None, None, ("tx", "ty")),
        P("traj", None, ("tx", "ty")),
        P(), P(), P(), P(), P(), P(),
    )
    return jax.shard_map(
        make_body(ring_size(mesh)), mesh=mesh, in_specs=in_specs, out_specs=out_specs, check_vma=False
    )
```

```python
import functools

import jax
import jax.numpy as jnp
from jax import lax
from jax.experimental import pallas as pl
from jax.experimental.pallas import tpu as pltpu
from jax.sharding import PartitionSpec as P

F32 = jnp.float32
BF16 = jnp.bfloat16
courant = 0.1
slope_gain = 0.25
HALO = 4
RING = ("tx", "ty")
Y_ORDER = (0, 2, 1, 3)


def split(x):
    hi = x.astype(BF16)
    return hi, (x - hi.astype(F32)).astype(BF16)


def split3(x):
    hi = x.astype(BF16)
    rest = x - hi.astype(F32)
    mid = rest.astype(BF16)
    return hi, mid, (rest - mid.astype(F32)).astype(BF16)


def six(parts, ones):
    hi, mid, low = parts
    return rows(hi, mid, low, hi, mid, hi, ones)


def dot(a, b):
    return lax.dot_general(a, b, (((1,), (0,)), ((), ())), preferred_element_type=F32)


def dot_nt(a, b):
    return lax.dot_general(a, b, (((1,), (1,)), ((), ())), preferred_element_type=F32)


def exact(a, b, nt=False):
    dims = (((1,), (1 if nt else 0,)), ((), ()))
    return lax.dot_general(a, b, dims, preferred_element_type=F32, precision=lax.Precision.HIGHEST)


def rows(*parts):
    return jnp.concatenate(parts, 0)


def lanes(*parts):
    return jnp.concatenate(parts, 1)


def roll(v, amount):
    return pltpu.roll(v, amount % v.shape[1], 1)


def halves_at(lead, at):
    return [tuple(lead) + (t, at, slice(None)) for t in range(2)]


def get(ref, lead, at):
    return lanes(*[ref[where] for where in halves_at(lead, at)])


def put(ref, lead, at, value):
    for t, where in enumerate(halves_at(lead, at)):
        ref[where] = value[:, 128 * t : 128 * t + 128]


def face_states(cells, gates):
    below, here, above, above2 = cells
    slope_left = [above[c] - below[c] for c in range(4)]
    slope_right = [above2[c] - here[c] for c in range(4)]
    left = [here[c] + slope_gain * gates[c] * slope_left[c] for c in range(4)]
    right = [above[c] - slope_gain * gates[4 + c] * slope_right[c] for c in range(4)]
    return slope_left, slope_right, left, right


def flux_of(left, right):
    u_left = left[1] * (1.0 / left[0])
    u_right = right[1] * (1.0 / right[0])
    speed = 0.5 * jnp.maximum(jnp.abs(u_left), jnp.abs(u_right)) + 0.5
    physical = (
        left[1] + right[1],
        left[1] * u_left + left[0] + (right[1] * u_right + right[0]),
        left[2] * u_left + right[2] * u_right,
        left[3] * u_left + right[3] * u_right,
    )
    return [0.5 * physical[c] - speed * (right[c] - left[c]) for c in range(4)]


def flux_back(cells, gates, cot):
    slope_left, slope_right, left, right = face_states(cells, gates)
    inv_left = 1.0 / left[0]
    inv_right = 1.0 / right[0]
    u_left = left[1] * inv_left
    u_right = right[1] * inv_right
    abs_left = jnp.abs(u_left)
    abs_right = jnp.abs(u_right)
    half = [0.5 * v for v in cot]
    speed = jnp.maximum(abs_left, abs_right) + 1.0
    d_speed = half[0] * (left[0] - right[0])
    for c in range(1, 4):
        d_speed = d_speed + half[c] * (left[c] - right[c])
    share_left = jnp.where(abs_left > abs_right, 1.0, jnp.where(abs_left < abs_right, 0.0, 0.5))
    d_abs_left = d_speed * share_left
    d_abs_right = d_speed - d_abs_left

    def one_side(state, inv, u, d_abs, sign):
        signed = jnp.where(u > 0.0, d_abs, jnp.where(u < 0.0, -d_abs, 0.0))
        d_u = half[1] * state[1] + half[2] * state[2] + half[3] * state[3] + signed
        d_u = d_u * inv
        visc = [sign * (speed * half[c]) for c in range(4)]
        return (
            half[1] - d_u * u + visc[0],
            half[0] + half[1] * u + d_u + visc[1],
            half[2] * u + visc[2],
            half[3] * u + visc[3],
        )

    d_left = one_side(left, inv_left, u_left, d_abs_left, 1.0)
    d_right = one_side(right, inv_right, u_right, d_abs_right, -1.0)
    scaled_left = [slope_gain * v for v in d_left]
    scaled_right = [slope_gain * v for v in d_right]
    d_gates = [scaled_left[c] * slope_left[c] for c in range(4)]
    d_gates += [-(scaled_right[c] * slope_right[c]) for c in range(4)]
    minus_below = [gates[c] * scaled_left[c] for c in range(4)]
    minus_above2 = [gates[4 + c] * scaled_right[c] for c in range(4)]
    to_here = [d_left[c] + minus_above2[c] for c in range(4)]
    to_above = [d_right[c] + minus_below[c] for c in range(4)]
    return d_gates, minus_below, to_here, to_above, minus_above2


def index(shape, axis):
    return lax.broadcasted_iota(jnp.int32, shape, axis)


def indicator(condition, dtype=F32):
    return jnp.where(condition, 1.0, 0.0).astype(F32).astype(dtype)


def fill_weights(given, filled):
    w_in, b_in, w_mid, b_mid, w_out, b_out = [ref[...] for ref in given]
    w_x, w_y, w_m, w_o, w_ot, w_mt, w_xt, w_yt = filled

    def bias_columns(bias, count, depth):
        parts = split3(jnp.broadcast_to(bias, (16, count)))
        r = index((16, count), 0)
        stacked = jnp.zeros((16, count), F32)
        for at in range(3):
            stacked = jnp.where(r == at, parts[at].astype(F32), stacked)
        below = jnp.zeros((depth, count), BF16)
        unit = indicator(index((count, count), 0) == index((count, count), 1), BF16)
        return dot_nt(unit, rows(below, stacked.astype(BF16)))

    def spread(parts, owners, block, columns, offset=0):
        count = parts[0].shape[1]
        r, k = index((count, columns), 0), index((count, columns), 1)
        total = None
        for at, part in enumerate(parts):
            inside = jnp.logical_and(k >= owners[at][0] * block, k < owners[at][1] * block)
            where = jnp.logical_and(inside, k % block == r + offset)
            piece = dot(part, indicator(where, BF16))
            total = piece if total is None else total + piece
        return total

    sixfold = ((0, 3), (3, 5), (5, 6))
    threefold = ((0, 2), (2, 3))
    for ref, weight, bias in ((w_x, w_in, b_in), (w_m, w_mid, b_mid), (w_o, w_out, b_out)):
        units, count = weight.shape
        value = spread(split3(weight), sixfold, count, 6 * count + 16)
        ref[...] = (value + bias_columns(bias, units, 6 * count)).astype(BF16)
    in_parts = split3(w_in)
    in_bias = bias_columns(b_in, 32, 192)
    for face in range(4):
        value = spread(in_parts, sixfold, 32, 208, 4 * face) + in_bias
        w_y[32 * face : 32 * face + 32, :] = value.astype(BF16)

    def turned(weight, lines):
        units = weight.shape[1]
        r, k = index((lines * units, units), 0), index((lines * units, units), 1)
        chosen = indicator(r % units == k, BF16)
        return [dot_nt(chosen, part).astype(BF16) for part in split(weight)]

    for ref, weight in ((w_ot, w_out), (w_mt, w_mid)):
        gates, units = weight.shape
        parts = turned(weight, 2)
        shape = (2 * units, 6 * gates)
        r, k = index(shape, 0), index(shape, 1)
        value = spread(parts, ((0, 4), (4, 6)), gates, 6 * gates)
        ref[...] = jnp.where((k // gates) % 2 == r // units, value, 0.0).astype(BF16)
    w_xt[...] = spread(turned(w_in, 1), threefold, 32, 96).astype(BF16)
    total = None
    for face in range(4):
        r, k = index((32, 16), 0), index((32, 16), 1)
        chosen = indicator(r == k + 4 * face, BF16)
        parts = [dot_nt(chosen, part).astype(BF16) for part in split(w_in)]
        value = spread(parts, threefold, 128, 384, 32 * face)
        total = value if total is None else total + value
    w_yt[...] = total.astype(BF16)


def kernel(
    density, momentum, tracer, cotangent, halo,
    w_in, b_in, w_mid, b_mid, w_out, b_out,
    g_density, g_momentum, g_tracer, packed,
    nat, cot, mid, mid_hi, mid_lo, mid_lo2,
    h1_hi, h1_lo, h2_hi, h2_lo, t_hi, t_lo, gate_x,
    face, d_mix, out_nat,
    xi, gi, di, mi, zi,
    acc_x, acc_y, acc_m, acc_o,
    w_x, w_y, w_m, w_o, w_ot, w_mt, w_xt, w_yt,
):
    width = nat.shape[2]
    own = density.shape[2]
    blocks = own // 8
    ones = jnp.ones((16, width), BF16)
    fill_weights(
        (w_in, b_in, w_mid, b_mid, w_out, b_out), (w_x, w_y, w_m, w_o, w_ot, w_mt, w_xt, w_yt)
    )

    for c in range(4):
        if c == 0:
            source = density[0]
        elif c == 3:
            source = tracer[0]
        else:
            source = momentum[0, c - 1]
        nat[c, 8 : 8 + own, :] = source.T
        nat[c, 0:8, :] = halo[c]
        put(cot, (c,), pl.ds(8, own), cotangent[0, c].T)
        put(cot, (c,), pl.ds(0, 8), halo[4 + c])
        put(cot, (c,), pl.ds(8 + own, 8), halo[4 + c])
    acc_x[...] = jnp.zeros_like(acc_x)
    acc_y[...] = jnp.zeros_like(acc_y)
    acc_m[...] = jnp.zeros_like(acc_m)
    acc_o[...] = jnp.zeros_like(acc_o)

    def upper_layers(first):
        first_parts = split3(first)
        seconds, gate_rows = [], []
        for line in range(4):
            at = slice(32 * line, 32 * line + 32)
            operand = six([part[at] for part in first_parts], ones)
            second = split3(jnp.tanh(dot(w_m[...], operand)))
            seconds.append(second)
            gate_rows.append(jnp.tanh(dot(w_o[...], six(second, ones))))
        return (
            first_parts[0],
            first_parts[1],
            rows(*[v[0] for v in seconds]),
            rows(*[v[1] for v in seconds]),
            rows(*gate_rows),
        )

    def limiter_back(gates, d_gates, load_first, load_second):
        for g in range(8):
            put(di, (), pl.ds(g, 8, stride=8), d_gates[g] * (1.0 - gates[g] * gates[g]))
        d_first, mid_lhs, mid_rhs, out_lhs, out_rhs = [], [], [], [], []
        for pair in range(4):
            o_hi, o_lo = split(get(di, (), pl.ds(16 * pair, 16)))
            s_hi, s_lo = load_second(pair)
            f_hi, f_lo = load_first(pair)
            second = s_hi.astype(F32) + s_lo.astype(F32)
            d_second = dot(w_ot[...], rows(o_hi, o_lo, o_hi)) * (1.0 - second * second)
            m_hi, m_lo = split(d_second)
            first = f_hi.astype(F32) + f_lo.astype(F32)
            d_one = dot(w_mt[...], rows(m_hi, m_lo, m_hi)) * (1.0 - first * first)
            d_first.append(split(d_one))
            for line in range(2):
                at = slice(32 * line, 32 * line + 32)
                mid_lhs.append(rows(m_hi[at], m_lo[at]))
                mid_rhs.append(rows(f_hi[at], f_lo[at], ones))
            out_lhs.append(rows(o_hi, o_lo))
            out_rhs.append(rows(s_hi, s_lo, ones))
        acc_m[...] += dot_nt(lanes(*mid_lhs), lanes(*mid_rhs))
        acc_o[...] += dot_nt(lanes(*out_lhs), lanes(*out_rhs))
        return d_first

    def x_forward(b, carry):
        n0 = pl.multiple_of(8 * b, 8)
        here = [nat[c, pl.ds(n0, 8), :] for c in range(4)]
        cells = [[roll(v, 1) for v in here], here, [roll(v, -1) for v in here], [roll(v, -2) for v in here]]
        for s in range(4):
            for c in range(4):
                put(xi, (), pl.ds(4 * s + c, 8, stride=16), cells[s][c])
        for q in range(2):
            window = split3(get(xi, (), pl.ds(64 * q, 64)))
            at = pl.ds(pl.multiple_of(128 * b + 64 * q, 64), 64)
            t_hi[at, :] = window[0]
            t_lo[at, :] = window[1]
            firsts = []
            for line in range(4):
                at = slice(16 * line, 16 * line + 16)
                firsts.append(dot(w_x[...], six([part[at] for part in window], ones)))
            first = jnp.tanh(rows(*firsts))
            f_hi, f_lo, s_hi, s_lo, gate_rows = upper_layers(first)
            at = pl.ds(pl.multiple_of(256 * b + 128 * q, 128), 128)
            h1_hi[at, :] = f_hi
            h1_lo[at, :] = f_lo
            h2_hi[at, :] = s_hi
            h2_lo[at, :] = s_lo
            put(gi, (), pl.ds(32 * q, 32), gate_rows)
        gates = [get(gi, (), pl.ds(g, 8, stride=8)) for g in range(8)]
        for g in range(8):
            gate_x[g, pl.ds(n0, 8), :] = gates[g]
        _, _, left, right = face_states(cells, gates)
        fluxes = flux_of(left, right)
        for c in range(4):
            value = here[c] - courant * (fluxes[c] - roll(fluxes[c], 1))
            put(mid, (c,), pl.ds(n0, 8), value)
            put(mi, (), pl.ds(Y_ORDER[c], 8, stride=4), value)
        at = pl.ds(pl.multiple_of(32 * b, 32), 32)
        for ref, part in zip((mid_hi, mid_lo, mid_lo2), split3(get(mi, (), pl.ds(0, 32)))):
            ref[at, :] = part
        return carry

    lax.fori_loop(0, blocks + 1, x_forward, 0)
    mid[:, :, 8 + own : 16 + own, :] = mid[:, :, 0:8, :]
    for ref in (mid_hi, mid_lo, mid_lo2):
        ref[4 * own + 32 : 4 * own + 64, :] = ref[0:32, :]
    d_mix[:, 0:16, :] = jnp.zeros((2, 16, 128), F32)

    def y_sweep(b, carry):
        n0 = pl.multiple_of(8 * b, 8)
        saved, windows = [], []
        for q in range(2):
            at = pl.ds(pl.multiple_of(32 * b + 16 * q, 16), 32)
            window = mid_hi[at, :], mid_lo[at, :], mid_lo2[at, :]
            windows.append(rows(window[0], window[1], ones))
            first = jnp.tanh(dot(w_y[...], six(window, ones)))
            parts = upper_layers(first)
            saved.append(parts)
            put(gi, (), pl.ds(32 * q, 32), parts[4])
        gates = [get(gi, (), pl.ds(g, 8, stride=8)) for g in range(8)]
        cells = [[get(mid, (c,), pl.ds(n0 + k, 8)) for c in Y_ORDER] for k in range(4)]
        cots = [courant * (get(cot, (c,), pl.ds(n0 + 2, 8)) - get(cot, (c,), pl.ds(n0 + 1, 8))) for c in Y_ORDER]
        d_gates, minus_below, to_here, to_above, minus_above2 = flux_back(cells, gates, cots)
        for c in range(4):
            to = Y_ORDER[c]
            put(face, (to,), pl.ds(n0, 8), minus_below[c])
            put(face, (4 + to,), pl.ds(n0, 8), to_here[c])
            put(face, (8 + to,), pl.ds(n0, 8), to_above[c])
            put(face, (12 + to,), pl.ds(n0, 8), minus_above2[c])

        def load(part):
            def of(pair):
                at = slice(64 * (pair % 2), 64 * (pair % 2) + 64)
                return saved[pair // 2][part][at], saved[pair // 2][part + 1][at]
            return of

        d_first = limiter_back(gates, d_gates, load(0), load(2))
        outs, right_side = [], []
        for q in range(2):
            hi = rows(d_first[2 * q][0], d_first[2 * q + 1][0])
            lo = rows(d_first[2 * q][1], d_first[2 * q + 1][1])
            outs.append(dot(w_yt[...], rows(hi, lo, hi)))
            right_side.append(rows(hi, lo))
        at = pl.multiple_of(32 * b, 32)
        put(d_mix, (), pl.ds(at, 16), get(d_mix, (), pl.ds(at, 16)) + outs[0][:16])
        put(d_mix, (), pl.ds(at + 16, 16), outs[0][16:] + outs[1][:16])
        put(d_mix, (), pl.ds(at + 32, 16), outs[1][16:])
        acc_y[...] += dot_nt(lanes(*windows), lanes(*right_side))

        @pl.when(b == 0)
        def _():
            acc_y[...] = jnp.zeros_like(acc_y)
            acc_m[...] = jnp.zeros_like(acc_m)
            acc_o[...] = jnp.zeros_like(acc_o)

        return carry

    lax.fori_loop(0, blocks + 1, y_sweep, 0)

    def x_back(b, carry):
        n0 = pl.multiple_of(8 * b, 8)
        gates = [gate_x[g, pl.ds(n0, 8), :] for g in range(8)]
        here = [nat[c, pl.ds(n0, 8), :] for c in range(4)]
        cells = [[roll(v, 1) for v in here], here, [roll(v, -1) for v in here], [roll(v, -2) for v in here]]
        back = []
        for c in range(4):
            value = get(cot, (c,), pl.ds(n0, 8)) + get(d_mix, (), pl.ds(4 * n0 + Y_ORDER[c], 8, stride=4))
            value = value + get(face, (4 + c,), pl.ds(n0 - 1, 8)) - get(face, (c,), pl.ds(n0, 8))
            value = value + get(face, (8 + c,), pl.ds(n0 - 2, 8)) - get(face, (12 + c,), pl.ds(n0 - 3, 8))
            back.append(value)
        cots = [courant * (roll(v, -1) - v) for v in back]
        d_gates, minus_below, to_here, to_above, minus_above2 = flux_back(cells, gates, cots)

        def load(hi_ref, lo_ref):
            def of(pair):
                at = pl.ds(pl.multiple_of(256 * b + 64 * pair, 64), 64)
                return hi_ref[at, :], lo_ref[at, :]
            return of

        d_first = limiter_back(gates, d_gates, load(h1_hi, h1_lo), load(h2_hi, h2_lo))
        left_side, right_side = [], []
        for line in range(8):
            at = pl.ds(pl.multiple_of(128 * b + 16 * line, 16), 16)
            left_side.append(rows(t_hi[at, :], t_lo[at, :], ones))
            at = slice(32 * (line % 2), 32 * (line % 2) + 32)
            hi, lo = [v[at] for v in d_first[line // 2]]
            right_side.append(rows(hi, lo))
            put(zi, (), pl.ds(16 * line, 16), dot(w_xt[...], rows(hi, lo, hi)))
        acc_x[...] += dot_nt(lanes(*left_side), lanes(*right_side))
        for c in range(4):
            parts = [get(zi, (), pl.ds(4 * s + c, 8, stride=16)) for s in range(4)]
            value = back[c] + to_here[c] + parts[1] + roll(parts[0] - minus_below[c], -1)
            value = value + roll(to_above[c] + parts[2], 1) + roll(parts[3] - minus_above2[c], 2)
            out_nat[c, pl.ds(pl.multiple_of(n0 - 8, 8), 8), :] = value
        return carry

    lax.fori_loop(1, blocks + 1, x_back, 0)

    g_density[0] = out_nat[0].T
    g_momentum[0, 0] = out_nat[1].T
    g_momentum[0, 1] = out_nat[2].T
    g_tracer[0] = out_nat[3].T

    r, k = index((24, 48), 0), index((24, 48), 1)
    pick = jnp.where(k < 32, k % 16, jnp.where(k == 32, 16, -1))
    first_x = exact(indicator(r == pick), acc_x[...])
    r, k = index((80, 256), 0), index((80, 256), 1)
    distance = (r // 4) % 8 - (k // 32) % 4
    rr, kk = index((24, 80), 0), index((24, 80), 1)
    masked = jnp.where(r == 64, acc_y[...], 0.0)
    first_y = exact(indicator(jnp.logical_and(rr == 16, kk == 64)), masked)
    for s in range(4):
        masked = jnp.where(jnp.logical_and(r < 64, distance == s), acc_y[...], 0.0)
        first_y = first_y + exact(indicator(jnp.logical_and(rr == 4 * s + kk % 4, kk < 64)), masked)

    def by_unit(shape, axis):
        return indicator(index(shape, axis) % 32 == index(shape, 1 - axis))

    first = exact(by_unit((32, 64), 1), first_x, nt=True) + exact(by_unit((32, 256), 1), first_y, nt=True)
    first_bias = exact(first_x, by_unit((64, 32), 0)) + exact(first_y, by_unit((256, 32), 0))
    r, k = index((24, 128), 0), index((24, 128), 1)
    total = exact(first, indicator(jnp.logical_and(k == r + 64, r < 16)))
    r, k = index((80, 128), 0), index((80, 128), 1)
    total = total + exact(exact(by_unit((32, 64), 1), acc_m[...]), indicator(jnp.logical_and(r % 32 == k, r < 64)))
    second_bias = exact(exact(indicator(index((8, 80), 1) == 64), acc_m[...], nt=True), by_unit((64, 32), 0))
    r, k = index((32, 144), 0), index((32, 144), 1)
    masked = jnp.where(jnp.logical_and(k < 128, (r // 8) % 2 == (k // 32) % 2), acc_o[...], 0.0)
    r, k = index((8, 32), 0), index((8, 32), 1)
    summed = exact(indicator(r == k % 8), masked)
    r, k = index((144, 128), 0), index((144, 128), 1)
    packed[0:32, :] = total
    packed[32:40, :] = exact(summed, indicator(jnp.logical_and(r % 32 == k, r < 128)))
    out_bias = exact(indicator(index((8, 144), 1) == 128), acc_o[...], nt=True)
    r, k = index((32, 128), 0), index((32, 128), 1)
    out_bias = exact(out_bias, indicator(r % 8 == k))
    r, k = index((32, 128), 0), index((32, 128), 1)
    wide = indicator(r == k)
    first_bias = exact(first_bias[16:24], wide)
    second_bias = exact(second_bias, wide)
    r = index((8, 128), 0)
    first_bias = jnp.broadcast_to(first_bias[0:1], (8, 128))
    packed[40:48, :] = jnp.where(
        r == 0, first_bias, jnp.where(r == 1, second_bias, jnp.where(r == 2, out_bias, 0.0))
    )


GROUPS = ("traj", "ty", "tx")


def reduce_kernel(sizes, mine, total, *scratch):
    count = len(sizes)
    slots, sends, receives = scratch[:count], scratch[count : 2 * count], scratch[2 * count :]
    mesh_ids = pl.DeviceIdType.MESH
    barrier = pltpu.get_barrier_semaphore()
    for axis, size in zip(GROUPS, sizes):
        here = lax.axis_index(axis)
        for step in range(1, size):
            peer = lax.rem(here + step, size)
            pl.semaphore_signal(barrier, inc=1, device_id={axis: peer}, device_id_type=mesh_ids)
    pl.semaphore_wait(barrier, sum(sizes) - count)
    value = mine[...]
    for at, (axis, size) in enumerate(zip(GROUPS, sizes)):
        here = lax.axis_index(axis)
        slots[at][here] = value
        copies = []
        for step in range(1, size):
            peer = lax.rem(here + step, size)
            copies.append(
                pltpu.make_async_remote_copy(
                    src_ref=slots[at].at[here],
                    dst_ref=slots[at].at[here],
                    send_sem=sends[at].at[step],
                    recv_sem=receives[at].at[step],
                    device_id={axis: peer},
                    device_id_type=mesh_ids,
                )
            )
        for copy in copies:
            copy.start()
        for copy in copies:
            copy.wait()
        value = slots[at][0]
        for other in range(1, size):
            value = value + slots[at][other]
    total[...] = value


def unpack_kernel(total, g_w_in, g_b_in, g_w_mid, g_b_mid, g_w_out, g_b_out):
    g_w_in[...] = total[0:32, 64:80]
    g_b_in[...] = total[40:41, 0:32]
    g_w_mid[...] = total[0:32, 0:32]
    g_b_mid[...] = total[41:42, 0:32]
    g_w_out[...] = total[32:40, 0:32]
    g_b_out[...] = total[42:43, 0:8]


def ring_size(mesh):
    return mesh.shape["tx"] * mesh.shape["ty"]


def make_body(size, sizes):
    def body(density, momentum, tracer, cotangent, w_in, b_in, w_mid, b_mid, w_out, b_out):
        own, width = density.shape[2], density.shape[1]
        states = jnp.concatenate([density[:, None], momentum, tracer[:, None], cotangent], 1)[0]
        low = jnp.swapaxes(states[:, :, :HALO], 1, 2)
        high = jnp.swapaxes(states[:, :, own - HALO :], 1, 2)
        from_right = lax.ppermute(low, RING, [((i + 1) % size, i) for i in range(size)])
        from_left = lax.ppermute(high, RING, [(i, (i + 1) % size) for i in range(size)])
        halo = jnp.concatenate([from_right, from_left], 1)
        biases = [b.reshape(1, -1) for b in (b_in, b_mid, b_out)]
        weights = (w_in, biases[0], w_mid, biases[1], w_out, biases[2])
        extra = own + 16
        lines = own + 8
        out = pl.pallas_call(
            kernel,
            out_shape=(
                jax.ShapeDtypeStruct(density.shape, F32),
                jax.ShapeDtypeStruct(momentum.shape, F32),
                jax.ShapeDtypeStruct(tracer.shape, F32),
                jax.ShapeDtypeStruct((48, 128), F32),
            ),
            in_specs=[pl.BlockSpec(memory_space=pltpu.VMEM)] * 11,
            out_specs=tuple([pl.BlockSpec(memory_space=pltpu.VMEM)] * 4),
            scratch_shapes=[
                pltpu.VMEM((4, lines, width), F32),
                pltpu.VMEM((4, 2, extra, 128), F32),
                pltpu.VMEM((4, 2, extra, 128), F32),
                pltpu.VMEM((4 * extra, width), BF16),
                pltpu.VMEM((4 * extra, width), BF16),
                pltpu.VMEM((4 * extra, width), BF16),
                pltpu.VMEM((32 * lines, width), BF16),
                pltpu.VMEM((32 * lines, width), BF16),
                pltpu.VMEM((32 * lines, width), BF16),
                pltpu.VMEM((32 * lines, width), BF16),
                pltpu.VMEM((16 * lines, width), BF16),
                pltpu.VMEM((16 * lines, width), BF16),
                pltpu.VMEM((8, lines, width), F32),
                pltpu.VMEM((16, 2, extra, 128), F32),
                pltpu.VMEM((2, 4 * extra, 128), F32),
                pltpu.VMEM((4, own, width), F32),
                pltpu.VMEM((2, 128, 128), F32),
                pltpu.VMEM((2, 64, 128), F32),
                pltpu.VMEM((2, 64, 128), F32),
                pltpu.VMEM((2, 32, 128), F32),
                pltpu.VMEM((2, 128, 128), F32),
                pltpu.VMEM((48, 64), F32),
                pltpu.VMEM((80, 256), F32),
                pltpu.VMEM((64, 80), F32),
                pltpu.VMEM((32, 144), F32),
                pltpu.VMEM((32, 112), BF16),
                pltpu.VMEM((128, 208), BF16),
                pltpu.VMEM((32, 208), BF16),
                pltpu.VMEM((8, 208), BF16),
                pltpu.VMEM((64, 48), BF16),
                pltpu.VMEM((64, 192), BF16),
                pltpu.VMEM((16, 96), BF16),
                pltpu.VMEM((32, 384), BF16),
            ],
            compiler_params=pltpu.CompilerParams(vmem_limit_bytes=60 * 1024 * 1024),
        )(density, momentum, tracer, cotangent, halo, *weights)
        in_vmem = pl.BlockSpec(memory_space=pltpu.VMEM)
        shape = (48, 128)
        total = pl.pallas_call(
            functools.partial(reduce_kernel, sizes),
            out_shape=jax.ShapeDtypeStruct(shape, F32),
            in_specs=[in_vmem],
            out_specs=in_vmem,
            scratch_shapes=[pltpu.VMEM((n,) + shape, F32) for n in sizes]
            + [pltpu.SemaphoreType.DMA((n,)) for n in sizes] * 2,
            compiler_params=pltpu.CompilerParams(collective_id=0, has_side_effects=True),
        )(out[3])
        totals = pl.pallas_call(
            unpack_kernel,
            out_shape=tuple(jax.ShapeDtypeStruct(w.shape, F32) for w in weights),
            in_specs=[in_vmem],
            out_specs=tuple([in_vmem] * 6),
        )(total)
        return (
            out[0],
            out[1],
            out[2],
            totals[0],
            totals[1].reshape(-1),
            totals[2],
            totals[3].reshape(-1),
            totals[4],
            totals[5].reshape(-1),
        )

    return body


def solution(mesh):
    in_specs = (
        P("traj", None, ("tx", "ty")),
        P("traj", None, None, ("tx", "ty")),
        P("traj", None, ("tx", "ty")),
        P("traj", None, None, ("tx", "ty")),
        P(), P(), P(), P(), P(), P(),
    )
    out_specs = (
        P("traj", None, ("tx", "ty")),
        P("traj", None, None, ("tx", "ty")),
        P("traj", None, ("tx", "ty")),
        P(), P(), P(), P(), P(), P(),
    )
    return jax.shard_map(
        make_body(ring_size(mesh), tuple(mesh.shape[axis] for axis in GROUPS)), mesh=mesh, in_specs=in_specs, out_specs=out_specs, check_vma=False
    )
```

```python
import functools

import jax
import jax.numpy as jnp
from jax import lax
from jax.experimental import pallas as pl
from jax.experimental.pallas import tpu as pltpu
from jax.sharding import PartitionSpec as P

F32 = jnp.float32
BF16 = jnp.bfloat16
courant = 0.1
slope_gain = 0.25
HALO = 4
RING = ("tx", "ty")
Y_ORDER = (0, 2, 1, 3)
STAGES = "bybybybyfbyfyfyfy"


def split(x):
    hi = x.astype(BF16)
    return hi, (x - hi.astype(F32)).astype(BF16)


def split3(x):
    hi = x.astype(BF16)
    rest = x - hi.astype(F32)
    mid = rest.astype(BF16)
    return hi, mid, (rest - mid.astype(F32)).astype(BF16)


def six(parts, ones):
    hi, mid, low = parts
    return rows(hi, mid, low, hi, mid, hi, ones)


def dot(a, b):
    return lax.dot_general(a, b, (((1,), (0,)), ((), ())), preferred_element_type=F32)


def dot_nt(a, b):
    return lax.dot_general(a, b, (((1,), (1,)), ((), ())), preferred_element_type=F32)


def exact(a, b, nt=False):
    dims = (((1,), (1 if nt else 0,)), ((), ()))
    return lax.dot_general(a, b, dims, preferred_element_type=F32, precision=lax.Precision.HIGHEST)


def rows(*parts):
    return jnp.concatenate(parts, 0)


def lanes(*parts):
    return jnp.concatenate(parts, 1)


def roll(v, amount):
    return pltpu.roll(v, amount % v.shape[1], 1)


def halves_at(lead, at):
    return [tuple(lead) + (t, at, slice(None)) for t in range(2)]


def get(ref, lead, at):
    return lanes(*[ref[where] for where in halves_at(lead, at)])


def put(ref, lead, at, value):
    for t, where in enumerate(halves_at(lead, at)):
        ref[where] = value[:, 128 * t : 128 * t + 128]


def face_states(cells, gates):
    below, here, above, above2 = cells
    slope_left = [above[c] - below[c] for c in range(4)]
    slope_right = [above2[c] - here[c] for c in range(4)]
    left = [here[c] + slope_gain * gates[c] * slope_left[c] for c in range(4)]
    right = [above[c] - slope_gain * gates[4 + c] * slope_right[c] for c in range(4)]
    return slope_left, slope_right, left, right


def flux_of(left, right):
    u_left = left[1] * (1.0 / left[0])
    u_right = right[1] * (1.0 / right[0])
    speed = 0.5 * jnp.maximum(jnp.abs(u_left), jnp.abs(u_right)) + 0.5
    physical = (
        left[1] + right[1],
        left[1] * u_left + left[0] + (right[1] * u_right + right[0]),
        left[2] * u_left + right[2] * u_right,
        left[3] * u_left + right[3] * u_right,
    )
    return [0.5 * physical[c] - speed * (right[c] - left[c]) for c in range(4)]


def flux_back(cells, gates, cot):
    slope_left, slope_right, left, right = face_states(cells, gates)
    inv_left = 1.0 / left[0]
    inv_right = 1.0 / right[0]
    u_left = left[1] * inv_left
    u_right = right[1] * inv_right
    abs_left = jnp.abs(u_left)
    abs_right = jnp.abs(u_right)
    half = [0.5 * v for v in cot]
    speed = jnp.maximum(abs_left, abs_right) + 1.0
    d_speed = half[0] * (left[0] - right[0])
    for c in range(1, 4):
        d_speed = d_speed + half[c] * (left[c] - right[c])
    share_left = jnp.where(abs_left > abs_right, 1.0, jnp.where(abs_left < abs_right, 0.0, 0.5))
    d_abs_left = d_speed * share_left
    d_abs_right = d_speed - d_abs_left

    def one_side(state, inv, u, d_abs, sign):
        signed = jnp.where(u > 0.0, d_abs, jnp.where(u < 0.0, -d_abs, 0.0))
        d_u = half[1] * state[1] + half[2] * state[2] + half[3] * state[3] + signed
        d_u = d_u * inv
        visc = [sign * (speed * half[c]) for c in range(4)]
        return (
            half[1] - d_u * u + visc[0],
            half[0] + half[1] * u + d_u + visc[1],
            half[2] * u + visc[2],
            half[3] * u + visc[3],
        )

    d_left = one_side(left, inv_left, u_left, d_abs_left, 1.0)
    d_right = one_side(right, inv_right, u_right, d_abs_right, -1.0)
    scaled_left = [slope_gain * v for v in d_left]
    scaled_right = [slope_gain * v for v in d_right]
    d_gates = [scaled_left[c] * slope_left[c] for c in range(4)]
    d_gates += [-(scaled_right[c] * slope_right[c]) for c in range(4)]
    minus_below = [gates[c] * scaled_left[c] for c in range(4)]
    minus_above2 = [gates[4 + c] * scaled_right[c] for c in range(4)]
    to_here = [d_left[c] + minus_above2[c] for c in range(4)]
    to_above = [d_right[c] + minus_below[c] for c in range(4)]
    return d_gates, minus_below, to_here, to_above, minus_above2


def index(shape, axis):
    return lax.broadcasted_iota(jnp.int32, shape, axis)


def indicator(condition, dtype=F32):
    return jnp.where(condition, 1.0, 0.0).astype(F32).astype(dtype)


def fill_weights(given, filled):
    w_in, b_in, w_mid, b_mid, w_out, b_out = [ref[...] for ref in given]
    w_x, w_y, w_m, w_o, w_ot, w_mt, w_xt, w_yt = filled

    def bias_columns(bias, count, depth):
        parts = split3(jnp.broadcast_to(bias, (16, count)))
        r = index((16, count), 0)
        stacked = jnp.zeros((16, count), F32)
        for at in range(3):
            stacked = jnp.where(r == at, parts[at].astype(F32), stacked)
        below = jnp.zeros((depth, count), BF16)
        unit = indicator(index((count, count), 0) == index((count, count), 1), BF16)
        return dot_nt(unit, rows(below, stacked.astype(BF16)))

    def spread(parts, owners, block, columns, offset=0):
        count = parts[0].shape[1]
        r, k = index((count, columns), 0), index((count, columns), 1)
        total = None
        for at, part in enumerate(parts):
            inside = jnp.logical_and(k >= owners[at][0] * block, k < owners[at][1] * block)
            where = jnp.logical_and(inside, k % block == r + offset)
            piece = dot(part, indicator(where, BF16))
            total = piece if total is None else total + piece
        return total

    sixfold = ((0, 3), (3, 5), (5, 6))
    threefold = ((0, 2), (2, 3))
    for ref, weight, bias in ((w_x, w_in, b_in), (w_m, w_mid, b_mid), (w_o, w_out, b_out)):
        units, count = weight.shape
        value = spread(split3(weight), sixfold, count, 6 * count + 16)
        ref[...] = (value + bias_columns(bias, units, 6 * count)).astype(BF16)
    in_parts = split3(w_in)
    in_bias = bias_columns(b_in, 32, 192)
    for face in range(4):
        value = spread(in_parts, sixfold, 32, 208, 4 * face) + in_bias
        w_y[32 * face : 32 * face + 32, :] = value.astype(BF16)

    def turned(weight, lines):
        units = weight.shape[1]
        r, k = index((lines * units, units), 0), index((lines * units, units), 1)
        chosen = indicator(r % units == k, BF16)
        return [dot_nt(chosen, part).astype(BF16) for part in split(weight)]

    for ref, weight in ((w_ot, w_out), (w_mt, w_mid)):
        gates, units = weight.shape
        parts = turned(weight, 2)
        shape = (2 * units, 6 * gates)
        r, k = index(shape, 0), index(shape, 1)
        value = spread(parts, ((0, 4), (4, 6)), gates, 6 * gates)
        ref[...] = jnp.where((k // gates) % 2 == r // units, value, 0.0).astype(BF16)
    w_xt[...] = spread(turned(w_in, 1), threefold, 32, 96).astype(BF16)
    total = None
    for face in range(4):
        r, k = index((32, 16), 0), index((32, 16), 1)
        chosen = indicator(r == k + 4 * face, BF16)
        parts = [dot_nt(chosen, part).astype(BF16) for part in split(w_in)]
        value = spread(parts, threefold, 128, 384, 32 * face)
        total = value if total is None else total + value
    w_yt[...] = total.astype(BF16)


def kernel(
    density, momentum, tracer, cotangent, halo,
    w_in, b_in, w_mid, b_mid, w_out, b_out,
    g_density, g_momentum, g_tracer, packed,
    nat, cot, mid, mid_hi, mid_lo, mid_lo2,
    h1_hi, h1_lo, h2_hi, h2_lo, t_hi, t_lo, gate_x,
    face, d_mix, out_nat,
    xi, gi, gi_y, di, di_y, mi, zi,
    acc_x, acc_y, acc_m, acc_o, acc_my, acc_oy,
    w_x, w_y, w_m, w_o, w_ot, w_mt, w_xt, w_yt,
):
    width = nat.shape[2]
    own = density.shape[2]
    blocks = own // 8
    ones = jnp.ones((16, width), BF16)
    fill_weights(
        (w_in, b_in, w_mid, b_mid, w_out, b_out), (w_x, w_y, w_m, w_o, w_ot, w_mt, w_xt, w_yt)
    )

    for c in range(4):
        if c == 0:
            source = density[0]
        elif c == 3:
            source = tracer[0]
        else:
            source = momentum[0, c - 1]
        nat[c, 8 : 8 + own, :] = source.T
        nat[c, 0:8, :] = halo[c]
        nat[c, 8 + own : 16 + own, :] = halo[c]
        put(cot, (c,), pl.ds(8, own), cotangent[0, c].T)
        put(cot, (c,), pl.ds(0, 8), halo[4 + c])
        put(cot, (c,), pl.ds(8 + own, 8), halo[4 + c])
    acc_x[...] = jnp.zeros_like(acc_x)
    acc_y[...] = jnp.zeros_like(acc_y)
    acc_m[...] = jnp.zeros_like(acc_m)
    acc_o[...] = jnp.zeros_like(acc_o)
    acc_my[...] = jnp.zeros_like(acc_my)
    acc_oy[...] = jnp.zeros_like(acc_oy)

    def middle(pre):
        firsts = [split3(jnp.tanh(v)) for v in pre]
        return firsts, [dot(w_m[...], six(v, ones)) for v in firsts]

    def output(pre):
        seconds = [split3(jnp.tanh(v)) for v in pre]
        return seconds, [dot(w_o[...], six(v, ones)) for v in seconds]

    def natural_gates(pre, gi):
        for line in range(8):
            put(gi, (), pl.ds(8 * line, 8), jnp.tanh(pre[line]))
        return [get(gi, (), pl.ds(g, 8, stride=8)) for g in range(8)]

    def back_output(gates, d_gates, di, load_second):
        for g in range(8):
            put(di, (), pl.ds(g, 8, stride=8), d_gates[g] * (1.0 - gates[g] * gates[g]))
        outs, pres = [], []
        for pair in range(4):
            o_hi, o_lo = split(get(di, (), pl.ds(16 * pair, 16)))
            outs.append((o_hi, o_lo))
            pres.append(dot(w_ot[...], rows(o_hi, o_lo, o_hi)))
        return outs, pres

    def back_through(pres, load, weight):
        parts, nexts = [], []
        for pair in range(4):
            s_hi, s_lo = load(pair)
            value = s_hi.astype(F32) + s_lo.astype(F32)
            part = split(pres[pair] * (1.0 - value * value))
            parts.append(part)
            if weight is not None:
                nexts.append(dot(weight[...], rows(part[0], part[1], part[0])))
        return parts, nexts

    def weight_sums(outs, d_second, load_first, load_second, acc_m, acc_o, valid):
        mid_lhs, mid_rhs, out_lhs, out_rhs = [], [], [], []
        for pair in range(4):
            f_hi, f_lo = load_first(pair)
            for line in range(2):
                at = slice(32 * line, 32 * line + 32)
                mid_lhs.append(rows(d_second[pair][0][at], d_second[pair][1][at]))
                mid_rhs.append(rows(f_hi[at], f_lo[at], ones))
            out_lhs.append(rows(*outs[pair]))
            out_rhs.append(rows(*load_second(pair), ones))
        acc_m[...] += jnp.where(valid, dot_nt(lanes(*mid_lhs), lanes(*mid_rhs)), 0.0)
        acc_o[...] += jnp.where(valid, dot_nt(lanes(*out_lhs), lanes(*out_rhs)), 0.0)

    def x_forward(b):
        n0 = pl.multiple_of(8 * b, 8)
        here = [nat[c, pl.ds(n0, 8), :] for c in range(4)]
        cells = [[roll(v, 1) for v in here], here, [roll(v, -1) for v in here], [roll(v, -2) for v in here]]
        for s in range(4):
            for c in range(4):
                put(xi, (), pl.ds(4 * s + c, 8, stride=16), cells[s][c])
        pre = []
        for line in range(8):
            window = split3(get(xi, (), pl.ds(16 * line, 16)))
            at = pl.ds(pl.multiple_of(128 * b + 16 * line, 16), 16)
            t_hi[at, :] = window[0]
            t_lo[at, :] = window[1]
            pre.append(dot(w_x[...], six(window, ones)))
        yield
        firsts, pre = middle(pre)
        for line in range(8):
            at = pl.ds(pl.multiple_of(256 * b + 32 * line, 32), 32)
            h1_hi[at, :] = firsts[line][0]
            h1_lo[at, :] = firsts[line][1]
        yield
        seconds, pre = output(pre)
        for line in range(8):
            at = pl.ds(pl.multiple_of(256 * b + 32 * line, 32), 32)
            h2_hi[at, :] = seconds[line][0]
            h2_lo[at, :] = seconds[line][1]
        yield
        gates = natural_gates(pre, gi)
        for g in range(8):
            gate_x[g, pl.ds(n0, 8), :] = gates[g]
        _, _, left, right = face_states(cells, gates)
        fluxes = flux_of(left, right)
        for c in range(4):
            value = here[c] - courant * (fluxes[c] - roll(fluxes[c], 1))
            put(mid, (c,), pl.ds(n0, 8), value)
            put(mi, (), pl.ds(Y_ORDER[c], 8, stride=4), value)
        at = pl.ds(pl.multiple_of(32 * b, 32), 32)
        for ref, part in zip((mid_hi, mid_lo, mid_lo2), split3(get(mi, (), pl.ds(0, 32)))):
            ref[at, :] = part
        yield

    d_mix[:, 0:16, :] = jnp.zeros((2, 16, 128), F32)

    def y_sweep(b, valid):
        n0 = pl.multiple_of(8 * b, 8)
        windows, pre = [], []
        for q in range(2):
            at = pl.ds(pl.multiple_of(32 * b + 16 * q, 16), 32)
            window = mid_hi[at, :], mid_lo[at, :], mid_lo2[at, :]
            windows.append(rows(window[0], window[1], ones))
            four = dot(w_y[...], six(window, ones))
            pre += [four[32 * line : 32 * line + 32] for line in range(4)]
        yield
        firsts, pre = middle(pre)
        yield
        seconds, pre = output(pre)
        yield
        gates = natural_gates(pre, gi_y)
        cells = [[get(mid, (c,), pl.ds(n0 + k, 8)) for c in Y_ORDER] for k in range(4)]
        cots = [courant * (get(cot, (c,), pl.ds(n0 + 2, 8)) - get(cot, (c,), pl.ds(n0 + 1, 8))) for c in Y_ORDER]
        d_gates, minus_below, to_here, to_above, minus_above2 = flux_back(cells, gates, cots)
        for c in range(4):
            to = Y_ORDER[c]
            put(face, (to,), pl.ds(n0, 8), minus_below[c])
            put(face, (4 + to,), pl.ds(n0, 8), to_here[c])
            put(face, (8 + to,), pl.ds(n0, 8), to_above[c])
            put(face, (12 + to,), pl.ds(n0, 8), minus_above2[c])

        def load(parts):
            return lambda pair: [rows(parts[2 * pair][k], parts[2 * pair + 1][k]) for k in range(2)]

        outs, pres = back_output(gates, d_gates, di_y, load(seconds))
        yield
        d_second, pres = back_through(pres, load(seconds), w_mt)
        yield
        d_first, _ = back_through(pres, load(firsts), None)
        combined, right_side = [], []
        for q in range(2):
            hi = rows(d_first[2 * q][0], d_first[2 * q + 1][0])
            lo = rows(d_first[2 * q][1], d_first[2 * q + 1][1])
            combined.append(dot(w_yt[...], rows(hi, lo, hi)))
            right_side.append(rows(hi, lo))
        yield
        weight_sums(outs, d_second, load(firsts), load(seconds), acc_my, acc_oy, valid)
        yield
        acc_y[...] += jnp.where(valid, dot_nt(lanes(*windows), lanes(*right_side)), 0.0)
        at = pl.multiple_of(32 * b, 32)
        put(d_mix, (), pl.ds(at, 16), get(d_mix, (), pl.ds(at, 16)) + combined[0][:16])
        put(d_mix, (), pl.ds(at + 16, 16), combined[0][16:] + combined[1][:16])
        put(d_mix, (), pl.ds(at + 32, 16), combined[1][16:])
        yield

    def x_back(b, valid):
        n0 = pl.multiple_of(8 * b, 8)
        gates = [gate_x[g, pl.ds(n0, 8), :] for g in range(8)]
        here = [nat[c, pl.ds(n0, 8), :] for c in range(4)]
        cells = [[roll(v, 1) for v in here], here, [roll(v, -1) for v in here], [roll(v, -2) for v in here]]
        back = []
        for c in range(4):
            value = get(cot, (c,), pl.ds(n0, 8)) + get(d_mix, (), pl.ds(4 * n0 + Y_ORDER[c], 8, stride=4))
            value = value + get(face, (4 + c,), pl.ds(n0 - 1, 8)) - get(face, (c,), pl.ds(n0, 8))
            value = value + get(face, (8 + c,), pl.ds(n0 - 2, 8)) - get(face, (12 + c,), pl.ds(n0 - 3, 8))
            back.append(value)
        cots = [courant * (roll(v, -1) - v) for v in back]
        d_gates, minus_below, to_here, to_above, minus_above2 = flux_back(cells, gates, cots)

        def load(hi_ref, lo_ref):
            def of(pair):
                at = pl.ds(pl.multiple_of(256 * b + 64 * pair, 64), 64)
                return hi_ref[at, :], lo_ref[at, :]
            return of

        first, second = load(h1_hi, h1_lo), load(h2_hi, h2_lo)
        outs, pres = back_output(gates, d_gates, di, second)
        direct = [
            (back[c] + to_here[c], minus_below[c], to_above[c], minus_above2[c]) for c in range(4)
        ]
        yield
        d_second, pres = back_through(pres, second, w_mt)
        yield
        d_first, _ = back_through(pres, first, None)
        left_side, right_side = [], []
        for line in range(8):
            at = pl.ds(pl.multiple_of(128 * b + 16 * line, 16), 16)
            left_side.append(rows(t_hi[at, :], t_lo[at, :], ones))
            at = slice(32 * (line % 2), 32 * (line % 2) + 32)
            hi, lo = [v[at] for v in d_first[line // 2]]
            right_side.append(rows(hi, lo))
            put(zi, (), pl.ds(16 * line, 16), dot(w_xt[...], rows(hi, lo, hi)))
        yield
        weight_sums(outs, d_second, first, second, acc_m, acc_o, valid)
        acc_x[...] += jnp.where(valid, dot_nt(lanes(*left_side), lanes(*right_side)), 0.0)
        yield
        for c in range(4):
            parts = [get(zi, (), pl.ds(4 * s + c, 8, stride=16)) for s in range(4)]
            value = direct[c][0] + parts[1] + roll(parts[0] - direct[c][1], -1)
            value = value + roll(direct[c][2] + parts[2], 1) + roll(parts[3] - direct[c][3], 2)
            out_nat[c, pl.ds(pl.multiple_of(n0 - 8, 8), 8), :] = value
        yield

    def step(i, carry):
        back = x_back(jnp.maximum(i - 3, 1), i >= 4)
        sweep = y_sweep(jnp.maximum(i - 2, 0), jnp.logical_and(i >= 3, i <= blocks + 2))
        ahead = x_forward(i)
        for stage in STAGES:
            next({"b": back, "y": sweep, "f": ahead}[stage])
        return carry

    lax.fori_loop(0, blocks + 4, step, 0)

    g_density[0] = out_nat[0].T
    g_momentum[0, 0] = out_nat[1].T
    g_momentum[0, 1] = out_nat[2].T
    g_tracer[0] = out_nat[3].T

    acc_m[...] += acc_my[...]
    acc_o[...] += acc_oy[...]
    r, k = index((24, 48), 0), index((24, 48), 1)
    pick = jnp.where(k < 32, k % 16, jnp.where(k == 32, 16, -1))
    first_x = exact(indicator(r == pick), acc_x[...])
    r, k = index((80, 256), 0), index((80, 256), 1)
    distance = (r // 4) % 8 - (k // 32) % 4
    rr, kk = index((24, 80), 0), index((24, 80), 1)
    masked = jnp.where(r == 64, acc_y[...], 0.0)
    first_y = exact(indicator(jnp.logical_and(rr == 16, kk == 64)), masked)
    for s in range(4):
        masked = jnp.where(jnp.logical_and(r < 64, distance == s), acc_y[...], 0.0)
        first_y = first_y + exact(indicator(jnp.logical_and(rr == 4 * s + kk % 4, kk < 64)), masked)

    def by_unit(shape, axis):
        return indicator(index(shape, axis) % 32 == index(shape, 1 - axis))

    first = exact(by_unit((32, 64), 1), first_x, nt=True) + exact(by_unit((32, 256), 1), first_y, nt=True)
    first_bias = exact(first_x, by_unit((64, 32), 0)) + exact(first_y, by_unit((256, 32), 0))
    r, k = index((24, 128), 0), index((24, 128), 1)
    total = exact(first, indicator(jnp.logical_and(k == r + 64, r < 16)))
    r, k = index((80, 128), 0), index((80, 128), 1)
    total = total + exact(exact(by_unit((32, 64), 1), acc_m[...]), indicator(jnp.logical_and(r % 32 == k, r < 64)))
    second_bias = exact(exact(indicator(index((8, 80), 1) == 64), acc_m[...], nt=True), by_unit((64, 32), 0))
    r, k = index((32, 144), 0), index((32, 144), 1)
    masked = jnp.where(jnp.logical_and(k < 128, (r // 8) % 2 == (k // 32) % 2), acc_o[...], 0.0)
    r, k = index((8, 32), 0), index((8, 32), 1)
    summed = exact(indicator(r == k % 8), masked)
    r, k = index((144, 128), 0), index((144, 128), 1)
    packed[0:32, :] = total
    packed[32:40, :] = exact(summed, indicator(jnp.logical_and(r % 32 == k, r < 128)))
    out_bias = exact(indicator(index((8, 144), 1) == 128), acc_o[...], nt=True)
    r, k = index((32, 128), 0), index((32, 128), 1)
    out_bias = exact(out_bias, indicator(r % 8 == k))
    r, k = index((32, 128), 0), index((32, 128), 1)
    wide = indicator(r == k)
    first_bias = exact(first_bias[16:24], wide)
    second_bias = exact(second_bias, wide)
    r = index((8, 128), 0)
    first_bias = jnp.broadcast_to(first_bias[0:1], (8, 128))
    packed[40:48, :] = jnp.where(
        r == 0, first_bias, jnp.where(r == 1, second_bias, jnp.where(r == 2, out_bias, 0.0))
    )


GROUPS = ("traj", "ty", "tx")


def reduce_kernel(sizes, mine, total, *scratch):
    count = len(sizes)
    slots, sends, receives = scratch[:count], scratch[count : 2 * count], scratch[2 * count :]
    mesh_ids = pl.DeviceIdType.MESH
    barrier = pltpu.get_barrier_semaphore()
    for axis, size in zip(GROUPS, sizes):
        here = lax.axis_index(axis)
        for step in range(1, size):
            peer = lax.rem(here + step, size)
            pl.semaphore_signal(barrier, inc=1, device_id={axis: peer}, device_id_type=mesh_ids)
    pl.semaphore_wait(barrier, sum(sizes) - count)
    value = mine[...]
    for at, (axis, size) in enumerate(zip(GROUPS, sizes)):
        here = lax.axis_index(axis)
        slots[at][here] = value
        copies = []
        for step in range(1, size):
            peer = lax.rem(here + step, size)
            copies.append(
                pltpu.make_async_remote_copy(
                    src_ref=slots[at].at[here],
                    dst_ref=slots[at].at[here],
                    send_sem=sends[at].at[step],
                    recv_sem=receives[at].at[step],
                    device_id={axis: peer},
                    device_id_type=mesh_ids,
                )
            )
        for copy in copies:
            copy.start()
        for copy in copies:
            copy.wait()
        value = slots[at][0]
        for other in range(1, size):
            value = value + slots[at][other]
    total[...] = value


def unpack_kernel(total, g_w_in, g_b_in, g_w_mid, g_b_mid, g_w_out, g_b_out):
    g_w_in[...] = total[0:32, 64:80]
    g_b_in[...] = total[40:41, 0:32]
    g_w_mid[...] = total[0:32, 0:32]
    g_b_mid[...] = total[41:42, 0:32]
    g_w_out[...] = total[32:40, 0:32]
    g_b_out[...] = total[42:43, 0:8]


def ring_size(mesh):
    return mesh.shape["tx"] * mesh.shape["ty"]


def make_body(size, sizes):
    def body(density, momentum, tracer, cotangent, w_in, b_in, w_mid, b_mid, w_out, b_out):
        own, width = density.shape[2], density.shape[1]
        states = jnp.concatenate([density[:, None], momentum, tracer[:, None], cotangent], 1)[0]
        low = jnp.swapaxes(states[:, :, :HALO], 1, 2)
        high = jnp.swapaxes(states[:, :, own - HALO :], 1, 2)
        from_right = lax.ppermute(low, RING, [((i + 1) % size, i) for i in range(size)])
        from_left = lax.ppermute(high, RING, [(i, (i + 1) % size) for i in range(size)])
        halo = jnp.concatenate([from_right, from_left], 1)
        biases = [b.reshape(1, -1) for b in (b_in, b_mid, b_out)]
        weights = (w_in, biases[0], w_mid, biases[1], w_out, biases[2])
        extra = own + 32
        lines = own + 32
        out = pl.pallas_call(
            kernel,
            out_shape=(
                jax.ShapeDtypeStruct(density.shape, F32),
                jax.ShapeDtypeStruct(momentum.shape, F32),
                jax.ShapeDtypeStruct(tracer.shape, F32),
                jax.ShapeDtypeStruct((48, 128), F32),
            ),
            in_specs=[pl.BlockSpec(memory_space=pltpu.VMEM)] * 11,
            out_specs=tuple([pl.BlockSpec(memory_space=pltpu.VMEM)] * 4),
            scratch_shapes=[
                pltpu.VMEM((4, lines, width), F32),
                pltpu.VMEM((4, 2, extra, 128), F32),
                pltpu.VMEM((4, 2, extra, 128), F32),
                pltpu.VMEM((4 * extra, width), BF16),
                pltpu.VMEM((4 * extra, width), BF16),
                pltpu.VMEM((4 * extra, width), BF16),
                pltpu.VMEM((32 * lines, width), BF16),
                pltpu.VMEM((32 * lines, width), BF16),
                pltpu.VMEM((32 * lines, width), BF16),
                pltpu.VMEM((32 * lines, width), BF16),
                pltpu.VMEM((16 * lines, width), BF16),
                pltpu.VMEM((16 * lines, width), BF16),
                pltpu.VMEM((8, lines, width), F32),
                pltpu.VMEM((16, 2, extra, 128), F32),
                pltpu.VMEM((2, 4 * extra, 128), F32),
                pltpu.VMEM((4, own, width), F32),
                pltpu.VMEM((2, 128, 128), F32),
                pltpu.VMEM((2, 64, 128), F32),
                pltpu.VMEM((2, 64, 128), F32),
                pltpu.VMEM((2, 64, 128), F32),
                pltpu.VMEM((2, 64, 128), F32),
                pltpu.VMEM((2, 32, 128), F32),
                pltpu.VMEM((2, 128, 128), F32),
                pltpu.VMEM((48, 64), F32),
                pltpu.VMEM((80, 256), F32),
                pltpu.VMEM((64, 80), F32),
                pltpu.VMEM((32, 144), F32),
                pltpu.VMEM((64, 80), F32),
                pltpu.VMEM((32, 144), F32),
                pltpu.VMEM((32, 112), BF16),
                pltpu.VMEM((128, 208), BF16),
                pltpu.VMEM((32, 208), BF16),
                pltpu.VMEM((8, 208), BF16),
                pltpu.VMEM((64, 48), BF16),
                pltpu.VMEM((64, 192), BF16),
                pltpu.VMEM((16, 96), BF16),
                pltpu.VMEM((32, 384), BF16),
            ],
            compiler_params=pltpu.CompilerParams(vmem_limit_bytes=60 * 1024 * 1024),
        )(density, momentum, tracer, cotangent, halo, *weights)
        in_vmem = pl.BlockSpec(memory_space=pltpu.VMEM)
        shape = (48, 128)
        total = pl.pallas_call(
            functools.partial(reduce_kernel, sizes),
            out_shape=jax.ShapeDtypeStruct(shape, F32),
            in_specs=[in_vmem],
            out_specs=in_vmem,
            scratch_shapes=[pltpu.VMEM((n,) + shape, F32) for n in sizes]
            + [pltpu.SemaphoreType.DMA((n,)) for n in sizes] * 2,
            compiler_params=pltpu.CompilerParams(collective_id=0, has_side_effects=True),
        )(out[3])
        totals = pl.pallas_call(
            unpack_kernel,
            out_shape=tuple(jax.ShapeDtypeStruct(w.shape, F32) for w in weights),
            in_specs=[in_vmem],
            out_specs=tuple([in_vmem] * 6),
        )(total)
        return (
            out[0],
            out[1],
            out[2],
            totals[0],
            totals[1].reshape(-1),
            totals[2],
            totals[3].reshape(-1),
            totals[4],
            totals[5].reshape(-1),
        )

    return body


def solution(mesh):
    in_specs = (
        P("traj", None, ("tx", "ty")),
        P("traj", None, None, ("tx", "ty")),
        P("traj", None, ("tx", "ty")),
        P("traj", None, None, ("tx", "ty")),
        P(), P(), P(), P(), P(), P(),
    )
    out_specs = (
        P("traj", None, ("tx", "ty")),
        P("traj", None, None, ("tx", "ty")),
        P("traj", None, ("tx", "ty")),
        P(), P(), P(), P(), P(), P(),
    )
    return jax.shard_map(
        make_body(ring_size(mesh), tuple(mesh.shape[axis] for axis in GROUPS)), mesh=mesh, in_specs=in_specs, out_specs=out_specs, check_vma=False
    )
```

```python
import functools

import jax
import jax.numpy as jnp
from jax import lax
from jax.experimental import pallas as pl
from jax.experimental.pallas import tpu as pltpu
from jax.sharding import PartitionSpec as P

F32 = jnp.float32
BF16 = jnp.bfloat16
courant = 0.1
slope_gain = 0.25
HALO = 4
Y_ORDER = (0, 2, 1, 3)
STAGES = "bybybybyfbyfyfyfy"


def split(x):
    hi = x.astype(BF16)
    return hi, (x - hi.astype(F32)).astype(BF16)


def split3(x):
    hi = x.astype(BF16)
    rest = x - hi.astype(F32)
    mid = rest.astype(BF16)
    return hi, mid, (rest - mid.astype(F32)).astype(BF16)


def six(parts, ones):
    hi, mid, low = parts
    return rows(hi, mid, low, hi, mid, hi, ones)


def dot(a, b):
    return lax.dot_general(a, b, (((1,), (0,)), ((), ())), preferred_element_type=F32)


def dot_nt(a, b):
    return lax.dot_general(a, b, (((1,), (1,)), ((), ())), preferred_element_type=F32)


def exact(a, b, nt=False):
    dims = (((1,), (1 if nt else 0,)), ((), ()))
    return lax.dot_general(a, b, dims, preferred_element_type=F32, precision=lax.Precision.HIGHEST)


def rows(*parts):
    return jnp.concatenate(parts, 0)


def lanes(*parts):
    return jnp.concatenate(parts, 1)


def roll(v, amount):
    return pltpu.roll(v, amount % v.shape[1], 1)


def halves_at(lead, at):
    return [tuple(lead) + (t, at, slice(None)) for t in range(2)]


def get(ref, lead, at):
    return lanes(*[ref[where] for where in halves_at(lead, at)])


def put(ref, lead, at, value):
    for t, where in enumerate(halves_at(lead, at)):
        ref[where] = value[:, 128 * t : 128 * t + 128]


def face_states(cells, gates):
    below, here, above, above2 = cells
    slope_left = [above[c] - below[c] for c in range(4)]
    slope_right = [above2[c] - here[c] for c in range(4)]
    left = [here[c] + slope_gain * gates[c] * slope_left[c] for c in range(4)]
    right = [above[c] - slope_gain * gates[4 + c] * slope_right[c] for c in range(4)]
    return slope_left, slope_right, left, right


def flux_of(left, right):
    u_left = left[1] * (1.0 / left[0])
    u_right = right[1] * (1.0 / right[0])
    speed = 0.5 * jnp.maximum(jnp.abs(u_left), jnp.abs(u_right)) + 0.5
    physical = (
        left[1] + right[1],
        left[1] * u_left + left[0] + (right[1] * u_right + right[0]),
        left[2] * u_left + right[2] * u_right,
        left[3] * u_left + right[3] * u_right,
    )
    return [0.5 * physical[c] - speed * (right[c] - left[c]) for c in range(4)]


def flux_back(cells, gates, cot):
    slope_left, slope_right, left, right = face_states(cells, gates)
    inv_left = 1.0 / left[0]
    inv_right = 1.0 / right[0]
    u_left = left[1] * inv_left
    u_right = right[1] * inv_right
    abs_left = jnp.abs(u_left)
    abs_right = jnp.abs(u_right)
    half = [0.5 * v for v in cot]
    speed = jnp.maximum(abs_left, abs_right) + 1.0
    d_speed = half[0] * (left[0] - right[0])
    for c in range(1, 4):
        d_speed = d_speed + half[c] * (left[c] - right[c])
    share_left = jnp.where(abs_left > abs_right, 1.0, jnp.where(abs_left < abs_right, 0.0, 0.5))
    d_abs_left = d_speed * share_left
    d_abs_right = d_speed - d_abs_left

    def one_side(state, inv, u, d_abs, sign):
        signed = jnp.where(u > 0.0, d_abs, jnp.where(u < 0.0, -d_abs, 0.0))
        d_u = half[1] * state[1] + half[2] * state[2] + half[3] * state[3] + signed
        d_u = d_u * inv
        visc = [sign * (speed * half[c]) for c in range(4)]
        return (
            half[1] - d_u * u + visc[0],
            half[0] + half[1] * u + d_u + visc[1],
            half[2] * u + visc[2],
            half[3] * u + visc[3],
        )

    d_left = one_side(left, inv_left, u_left, d_abs_left, 1.0)
    d_right = one_side(right, inv_right, u_right, d_abs_right, -1.0)
    scaled_left = [slope_gain * v for v in d_left]
    scaled_right = [slope_gain * v for v in d_right]
    d_gates = [scaled_left[c] * slope_left[c] for c in range(4)]
    d_gates += [-(scaled_right[c] * slope_right[c]) for c in range(4)]
    minus_below = [gates[c] * scaled_left[c] for c in range(4)]
    minus_above2 = [gates[4 + c] * scaled_right[c] for c in range(4)]
    to_here = [d_left[c] + minus_above2[c] for c in range(4)]
    to_above = [d_right[c] + minus_below[c] for c in range(4)]
    return d_gates, minus_below, to_here, to_above, minus_above2


def index(shape, axis):
    return lax.broadcasted_iota(jnp.int32, shape, axis)


def indicator(condition, dtype=F32):
    return jnp.where(condition, 1.0, 0.0).astype(F32).astype(dtype)


def fill_weights(given, filled):
    w_in, b_in, w_mid, b_mid, w_out, b_out = [ref[...] for ref in given]
    w_x, w_y, w_m, w_o, w_ot, w_mt, w_xt, w_yt = filled

    def bias_columns(bias, count, depth):
        parts = split3(jnp.broadcast_to(bias, (16, count)))
        r = index((16, count), 0)
        stacked = jnp.zeros((16, count), F32)
        for at in range(3):
            stacked = jnp.where(r == at, parts[at].astype(F32), stacked)
        below = jnp.zeros((depth, count), BF16)
        unit = indicator(index((count, count), 0) == index((count, count), 1), BF16)
        return dot_nt(unit, rows(below, stacked.astype(BF16)))

    def spread(parts, owners, block, columns, offset=0):
        count = parts[0].shape[1]
        r, k = index((count, columns), 0), index((count, columns), 1)
        total = None
        for at, part in enumerate(parts):
            inside = jnp.logical_and(k >= owners[at][0] * block, k < owners[at][1] * block)
            where = jnp.logical_and(inside, k % block == r + offset)
            piece = dot(part, indicator(where, BF16))
            total = piece if total is None else total + piece
        return total

    sixfold = ((0, 3), (3, 5), (5, 6))
    threefold = ((0, 2), (2, 3))
    for ref, weight, bias in ((w_x, w_in, b_in), (w_m, w_mid, b_mid), (w_o, w_out, b_out)):
        units, count = weight.shape
        value = spread(split3(weight), sixfold, count, 6 * count + 16)
        ref[...] = (value + bias_columns(bias, units, 6 * count)).astype(BF16)
    in_parts = split3(w_in)
    in_bias = bias_columns(b_in, 32, 192)
    for face in range(4):
        value = spread(in_parts, sixfold, 32, 208, 4 * face) + in_bias
        w_y[32 * face : 32 * face + 32, :] = value.astype(BF16)

    def turned(weight, lines):
        units = weight.shape[1]
        r, k = index((lines * units, units), 0), index((lines * units, units), 1)
        chosen = indicator(r % units == k, BF16)
        return [dot_nt(chosen, part).astype(BF16) for part in split(weight)]

    for ref, weight in ((w_ot, w_out), (w_mt, w_mid)):
        gates, units = weight.shape
        parts = turned(weight, 2)
        shape = (2 * units, 6 * gates)
        r, k = index(shape, 0), index(shape, 1)
        value = spread(parts, ((0, 4), (4, 6)), gates, 6 * gates)
        ref[...] = jnp.where((k // gates) % 2 == r // units, value, 0.0).astype(BF16)
    w_xt[...] = spread(turned(w_in, 1), threefold, 32, 96).astype(BF16)
    total = None
    for face in range(4):
        r, k = index((32, 16), 0), index((32, 16), 1)
        chosen = indicator(r == k + 4 * face, BF16)
        parts = [dot_nt(chosen, part).astype(BF16) for part in split(w_in)]
        value = spread(parts, threefold, 128, 384, 32 * face)
        total = value if total is None else total + value
    w_yt[...] = total.astype(BF16)


def kernel(
    density, momentum, tracer, cotangent, halo,
    w_in, b_in, w_mid, b_mid, w_out, b_out,
    g_density, g_momentum, g_tracer, packed,
    nat, cot, mid, mid_hi, mid_lo, mid_lo2,
    h1_hi, h1_lo, h2_hi, h2_lo, t_hi, t_lo, gate_x,
    face, d_mix, out_nat,
    xi, gi, gi_y, di, di_y, mi, zi,
    acc_x, acc_y, acc_m, acc_o, acc_my, acc_oy,
    w_x, w_y, w_m, w_o, w_ot, w_mt, w_xt, w_yt,
):
    width = nat.shape[2]
    own = density.shape[2]
    blocks = own // 8
    ones = jnp.ones((16, width), BF16)
    fill_weights(
        (w_in, b_in, w_mid, b_mid, w_out, b_out), (w_x, w_y, w_m, w_o, w_ot, w_mt, w_xt, w_yt)
    )

    for c in range(4):
        if c == 0:
            source = density[0]
        elif c == 3:
            source = tracer[0]
        else:
            source = momentum[0, c - 1]
        nat[c, 8 : 8 + own, :] = source.T
        for side in range(2):
            edge = halo[side, 4 * c : 4 * c + 4, :]
            nat[c, 4 * side : 4 * side + 4, :] = edge
            nat[c, 8 + own + 4 * side : 12 + own + 4 * side, :] = edge
        put(cot, (c,), pl.ds(8, own), cotangent[0, c].T)
        for side in range(2):
            edge = halo[side, 16 + 4 * c : 20 + 4 * c, :]
            put(cot, (c,), pl.ds(4 * side, 4), edge)
            put(cot, (c,), pl.ds(8 + own + 4 * side, 4), edge)
    acc_x[...] = jnp.zeros_like(acc_x)
    acc_y[...] = jnp.zeros_like(acc_y)
    acc_m[...] = jnp.zeros_like(acc_m)
    acc_o[...] = jnp.zeros_like(acc_o)
    acc_my[...] = jnp.zeros_like(acc_my)
    acc_oy[...] = jnp.zeros_like(acc_oy)

    def middle(pre):
        firsts = [split3(jnp.tanh(v)) for v in pre]
        return firsts, [dot(w_m[...], six(v, ones)) for v in firsts]

    def output(pre):
        seconds = [split3(jnp.tanh(v)) for v in pre]
        return seconds, [dot(w_o[...], six(v, ones)) for v in seconds]

    def natural_gates(pre, gi):
        for line in range(8):
            put(gi, (), pl.ds(8 * line, 8), jnp.tanh(pre[line]))
        return [get(gi, (), pl.ds(g, 8, stride=8)) for g in range(8)]

    def back_output(gates, d_gates, di, load_second):
        for g in range(8):
            put(di, (), pl.ds(g, 8, stride=8), d_gates[g] * (1.0 - gates[g] * gates[g]))
        outs, pres = [], []
        for pair in range(4):
            o_hi, o_lo = split(get(di, (), pl.ds(16 * pair, 16)))
            outs.append((o_hi, o_lo))
            pres.append(dot(w_ot[...], rows(o_hi, o_lo, o_hi)))
        return outs, pres

    def back_through(pres, load, weight):
        parts, nexts = [], []
        for pair in range(4):
            s_hi, s_lo = load(pair)
            value = s_hi.astype(F32) + s_lo.astype(F32)
            part = split(pres[pair] * (1.0 - value * value))
            parts.append(part)
            if weight is not None:
                nexts.append(dot(weight[...], rows(part[0], part[1], part[0])))
        return parts, nexts

    def weight_sums(outs, d_second, load_first, load_second, acc_m, acc_o, valid):
        mid_lhs, mid_rhs, out_lhs, out_rhs = [], [], [], []
        for pair in range(4):
            f_hi, f_lo = load_first(pair)
            for line in range(2):
                at = slice(32 * line, 32 * line + 32)
                mid_lhs.append(rows(d_second[pair][0][at], d_second[pair][1][at]))
                mid_rhs.append(rows(f_hi[at], f_lo[at], ones))
            out_lhs.append(rows(*outs[pair]))
            out_rhs.append(rows(*load_second(pair), ones))
        acc_m[...] += jnp.where(valid, dot_nt(lanes(*mid_lhs), lanes(*mid_rhs)), 0.0)
        acc_o[...] += jnp.where(valid, dot_nt(lanes(*out_lhs), lanes(*out_rhs)), 0.0)

    def x_forward(b):
        n0 = pl.multiple_of(8 * b, 8)
        here = [nat[c, pl.ds(n0, 8), :] for c in range(4)]
        cells = [[roll(v, 1) for v in here], here, [roll(v, -1) for v in here], [roll(v, -2) for v in here]]
        for s in range(4):
            for c in range(4):
                put(xi, (), pl.ds(4 * s + c, 8, stride=16), cells[s][c])
        pre = []
        for line in range(8):
            window = split3(get(xi, (), pl.ds(16 * line, 16)))
            at = pl.ds(pl.multiple_of(128 * b + 16 * line, 16), 16)
            t_hi[at, :] = window[0]
            t_lo[at, :] = window[1]
            pre.append(dot(w_x[...], six(window, ones)))
        yield
        firsts, pre = middle(pre)
        for line in range(8):
            at = pl.ds(pl.multiple_of(256 * b + 32 * line, 32), 32)
            h1_hi[at, :] = firsts[line][0]
            h1_lo[at, :] = firsts[line][1]
        yield
        seconds, pre = output(pre)
        for line in range(8):
            at = pl.ds(pl.multiple_of(256 * b + 32 * line, 32), 32)
            h2_hi[at, :] = seconds[line][0]
            h2_lo[at, :] = seconds[line][1]
        yield
        gates = natural_gates(pre, gi)
        for g in range(8):
            gate_x[g, pl.ds(n0, 8), :] = gates[g]
        _, _, left, right = face_states(cells, gates)
        fluxes = flux_of(left, right)
        for c in range(4):
            value = here[c] - courant * (fluxes[c] - roll(fluxes[c], 1))
            put(mid, (c,), pl.ds(n0, 8), value)
            put(mi, (), pl.ds(Y_ORDER[c], 8, stride=4), value)
        at = pl.ds(pl.multiple_of(32 * b, 32), 32)
        for ref, part in zip((mid_hi, mid_lo, mid_lo2), split3(get(mi, (), pl.ds(0, 32)))):
            ref[at, :] = part
        yield

    d_mix[:, 0:16, :] = jnp.zeros((2, 16, 128), F32)

    def y_sweep(b, valid):
        n0 = pl.multiple_of(8 * b, 8)
        windows, pre = [], []
        for q in range(2):
            at = pl.ds(pl.multiple_of(32 * b + 16 * q, 16), 32)
            window = mid_hi[at, :], mid_lo[at, :], mid_lo2[at, :]
            windows.append(rows(window[0], window[1], ones))
            four = dot(w_y[...], six(window, ones))
            pre += [four[32 * line : 32 * line + 32] for line in range(4)]
        yield
        firsts, pre = middle(pre)
        yield
        seconds, pre = output(pre)
        yield
        gates = natural_gates(pre, gi_y)
        cells = [[get(mid, (c,), pl.ds(n0 + k, 8)) for c in Y_ORDER] for k in range(4)]
        cots = [courant * (get(cot, (c,), pl.ds(n0 + 2, 8)) - get(cot, (c,), pl.ds(n0 + 1, 8))) for c in Y_ORDER]
        d_gates, minus_below, to_here, to_above, minus_above2 = flux_back(cells, gates, cots)
        for c in range(4):
            to = Y_ORDER[c]
            put(face, (to,), pl.ds(n0, 8), minus_below[c])
            put(face, (4 + to,), pl.ds(n0, 8), to_here[c])
            put(face, (8 + to,), pl.ds(n0, 8), to_above[c])
            put(face, (12 + to,), pl.ds(n0, 8), minus_above2[c])

        def load(parts):
            return lambda pair: [rows(parts[2 * pair][k], parts[2 * pair + 1][k]) for k in range(2)]

        outs, pres = back_output(gates, d_gates, di_y, load(seconds))
        yield
        d_second, pres = back_through(pres, load(seconds), w_mt)
        yield
        d_first, _ = back_through(pres, load(firsts), None)
        combined, right_side = [], []
        for q in range(2):
            hi = rows(d_first[2 * q][0], d_first[2 * q + 1][0])
            lo = rows(d_first[2 * q][1], d_first[2 * q + 1][1])
            combined.append(dot(w_yt[...], rows(hi, lo, hi)))
            right_side.append(rows(hi, lo))
        yield
        weight_sums(outs, d_second, load(firsts), load(seconds), acc_my, acc_oy, valid)
        yield
        acc_y[...] += jnp.where(valid, dot_nt(lanes(*windows), lanes(*right_side)), 0.0)
        at = pl.multiple_of(32 * b, 32)
        put(d_mix, (), pl.ds(at, 16), get(d_mix, (), pl.ds(at, 16)) + combined[0][:16])
        put(d_mix, (), pl.ds(at + 16, 16), combined[0][16:] + combined[1][:16])
        put(d_mix, (), pl.ds(at + 32, 16), combined[1][16:])
        yield

    def x_back(b, valid):
        n0 = pl.multiple_of(8 * b, 8)
        gates = [gate_x[g, pl.ds(n0, 8), :] for g in range(8)]
        here = [nat[c, pl.ds(n0, 8), :] for c in range(4)]
        cells = [[roll(v, 1) for v in here], here, [roll(v, -1) for v in here], [roll(v, -2) for v in here]]
        back = []
        for c in range(4):
            value = get(cot, (c,), pl.ds(n0, 8)) + get(d_mix, (), pl.ds(4 * n0 + Y_ORDER[c], 8, stride=4))
            value = value + get(face, (4 + c,), pl.ds(n0 - 1, 8)) - get(face, (c,), pl.ds(n0, 8))
            value = value + get(face, (8 + c,), pl.ds(n0 - 2, 8)) - get(face, (12 + c,), pl.ds(n0 - 3, 8))
            back.append(value)
        cots = [courant * (roll(v, -1) - v) for v in back]
        d_gates, minus_below, to_here, to_above, minus_above2 = flux_back(cells, gates, cots)

        def load(hi_ref, lo_ref):
            def of(pair):
                at = pl.ds(pl.multiple_of(256 * b + 64 * pair, 64), 64)
                return hi_ref[at, :], lo_ref[at, :]
            return of

        first, second = load(h1_hi, h1_lo), load(h2_hi, h2_lo)
        outs, pres = back_output(gates, d_gates, di, second)
        direct = [
            (back[c] + to_here[c], minus_below[c], to_above[c], minus_above2[c]) for c in range(4)
        ]
        yield
        d_second, pres = back_through(pres, second, w_mt)
        yield
        d_first, _ = back_through(pres, first, None)
        left_side, right_side = [], []
        for line in range(8):
            at = pl.ds(pl.multiple_of(128 * b + 16 * line, 16), 16)
            left_side.append(rows(t_hi[at, :], t_lo[at, :], ones))
            at = slice(32 * (line % 2), 32 * (line % 2) + 32)
            hi, lo = [v[at] for v in d_first[line // 2]]
            right_side.append(rows(hi, lo))
            put(zi, (), pl.ds(16 * line, 16), dot(w_xt[...], rows(hi, lo, hi)))
        yield
        weight_sums(outs, d_second, first, second, acc_m, acc_o, valid)
        acc_x[...] += jnp.where(valid, dot_nt(lanes(*left_side), lanes(*right_side)), 0.0)
        yield
        for c in range(4):
            parts = [get(zi, (), pl.ds(4 * s + c, 8, stride=16)) for s in range(4)]
            value = direct[c][0] + parts[1] + roll(parts[0] - direct[c][1], -1)
            value = value + roll(direct[c][2] + parts[2], 1) + roll(parts[3] - direct[c][3], 2)
            out_nat[c, pl.ds(pl.multiple_of(n0 - 8, 8), 8), :] = value
        yield

    def step(i, carry):
        back = x_back(jnp.maximum(i - 3, 1), i >= 4)
        sweep = y_sweep(jnp.maximum(i - 2, 0), jnp.logical_and(i >= 3, i <= blocks + 2))
        ahead = x_forward(i)
        for stage in STAGES:
            next({"b": back, "y": sweep, "f": ahead}[stage])
        return carry

    lax.fori_loop(0, blocks + 4, step, 0)

    g_density[0] = out_nat[0].T
    g_momentum[0, 0] = out_nat[1].T
    g_momentum[0, 1] = out_nat[2].T
    g_tracer[0] = out_nat[3].T

    acc_m[...] += acc_my[...]
    acc_o[...] += acc_oy[...]
    r, k = index((24, 48), 0), index((24, 48), 1)
    pick = jnp.where(k < 32, k % 16, jnp.where(k == 32, 16, -1))
    first_x = exact(indicator(r == pick), acc_x[...])
    r, k = index((80, 256), 0), index((80, 256), 1)
    distance = (r // 4) % 8 - (k // 32) % 4
    rr, kk = index((24, 80), 0), index((24, 80), 1)
    masked = jnp.where(r == 64, acc_y[...], 0.0)
    first_y = exact(indicator(jnp.logical_and(rr == 16, kk == 64)), masked)
    for s in range(4):
        masked = jnp.where(jnp.logical_and(r < 64, distance == s), acc_y[...], 0.0)
        first_y = first_y + exact(indicator(jnp.logical_and(rr == 4 * s + kk % 4, kk < 64)), masked)

    def by_unit(shape, axis):
        return indicator(index(shape, axis) % 32 == index(shape, 1 - axis))

    first = exact(by_unit((32, 64), 1), first_x, nt=True) + exact(by_unit((32, 256), 1), first_y, nt=True)
    first_bias = exact(first_x, by_unit((64, 32), 0)) + exact(first_y, by_unit((256, 32), 0))
    r, k = index((24, 128), 0), index((24, 128), 1)
    total = exact(first, indicator(jnp.logical_and(k == r + 64, r < 16)))
    r, k = index((80, 128), 0), index((80, 128), 1)
    total = total + exact(exact(by_unit((32, 64), 1), acc_m[...]), indicator(jnp.logical_and(r % 32 == k, r < 64)))
    second_bias = exact(exact(indicator(index((8, 80), 1) == 64), acc_m[...], nt=True), by_unit((64, 32), 0))
    r, k = index((32, 144), 0), index((32, 144), 1)
    masked = jnp.where(jnp.logical_and(k < 128, (r // 8) % 2 == (k // 32) % 2), acc_o[...], 0.0)
    r, k = index((8, 32), 0), index((8, 32), 1)
    summed = exact(indicator(r == k % 8), masked)
    r, k = index((144, 128), 0), index((144, 128), 1)
    packed[0:32, :] = total
    packed[32:40, :] = exact(summed, indicator(jnp.logical_and(r % 32 == k, r < 128)))
    out_bias = exact(indicator(index((8, 144), 1) == 128), acc_o[...], nt=True)
    r, k = index((32, 128), 0), index((32, 128), 1)
    out_bias = exact(out_bias, indicator(r % 8 == k))
    r, k = index((32, 128), 0), index((32, 128), 1)
    wide = indicator(r == k)
    first_bias = exact(first_bias[16:24], wide)
    second_bias = exact(second_bias, wide)
    r = index((8, 128), 0)
    first_bias = jnp.broadcast_to(first_bias[0:1], (8, 128))
    packed[40:48, :] = jnp.where(
        r == 0, first_bias, jnp.where(r == 1, second_bias, jnp.where(r == 2, out_bias, 0.0))
    )


def halo_kernel(size, inner, density, momentum, tracer, cotangent, halo, sent, landed, send_sem, recv_sem):
    mesh_ids = pl.DeviceIdType.MESH
    here = lax.axis_index("tx") * inner + lax.axis_index("ty")
    peers = []
    for step in (size - 1, 1):
        peer = lax.rem(here + step, size)
        peers.append({"tx": peer // inner, "ty": lax.rem(peer, inner)})
    barrier = pltpu.get_barrier_semaphore()
    for peer in peers:
        pl.semaphore_signal(barrier, inc=1, device_id=peer, device_id_type=mesh_ids)
    own = density.shape[2]
    for c in range(8):
        if c >= 4:
            source = cotangent[0, c - 4]
        elif c == 0:
            source = density[0]
        elif c == 3:
            source = tracer[0]
        else:
            source = momentum[0, c - 1]
        lines = source.T
        sent[0, 4 * c : 4 * c + 4, :] = lines[:HALO]
        sent[1, 4 * c : 4 * c + 4, :] = lines[own - HALO :]
    pl.semaphore_wait(barrier, 2)
    copies = [
        pltpu.make_async_remote_copy(
            src_ref=sent.at[side],
            dst_ref=landed.at[side],
            send_sem=send_sem.at[side],
            recv_sem=recv_sem.at[side],
            device_id=peers[side],
            device_id_type=mesh_ids,
        )
        for side in range(2)
    ]
    for copy in copies:
        copy.start()
    for copy in copies:
        copy.wait()
    halo[...] = landed[...]


GROUPS = ("traj", "ty", "tx")


def reduce_kernel(sizes, mine, total, *scratch):
    count = len(sizes)
    slots, sends, receives = scratch[:count], scratch[count : 2 * count], scratch[2 * count :]
    mesh_ids = pl.DeviceIdType.MESH
    barrier = pltpu.get_barrier_semaphore()
    for axis, size in zip(GROUPS, sizes):
        here = lax.axis_index(axis)
        for step in range(1, size):
            peer = lax.rem(here + step, size)
            pl.semaphore_signal(barrier, inc=1, device_id={axis: peer}, device_id_type=mesh_ids)
    pl.semaphore_wait(barrier, sum(sizes) - count)
    value = mine[...]
    for at, (axis, size) in enumerate(zip(GROUPS, sizes)):
        here = lax.axis_index(axis)
        slots[at][here] = value
        copies = []
        for step in range(1, size):
            peer = lax.rem(here + step, size)
            copies.append(
                pltpu.make_async_remote_copy(
                    src_ref=slots[at].at[here],
                    dst_ref=slots[at].at[here],
                    send_sem=sends[at].at[step],
                    recv_sem=receives[at].at[step],
                    device_id={axis: peer},
                    device_id_type=mesh_ids,
                )
            )
        for copy in copies:
            copy.start()
        for copy in copies:
            copy.wait()
        value = slots[at][0]
        for other in range(1, size):
            value = value + slots[at][other]
    total[...] = value


def unpack_kernel(total, g_w_in, g_b_in, g_w_mid, g_b_mid, g_w_out, g_b_out):
    g_w_in[...] = total[0:32, 64:80]
    g_b_in[...] = total[40:41, 0:32]
    g_w_mid[...] = total[0:32, 0:32]
    g_b_mid[...] = total[41:42, 0:32]
    g_w_out[...] = total[32:40, 0:32]
    g_b_out[...] = total[42:43, 0:8]


def ring_size(mesh):
    return mesh.shape["tx"] * mesh.shape["ty"]


def make_body(size, inner, sizes):
    def body(density, momentum, tracer, cotangent, w_in, b_in, w_mid, b_mid, w_out, b_out):
        own, width = density.shape[2], density.shape[1]
        in_vmem = pl.BlockSpec(memory_space=pltpu.VMEM)
        halo_shape = (2, 8 * HALO, width)
        halo = pl.pallas_call(
            functools.partial(halo_kernel, size, inner),
            out_shape=jax.ShapeDtypeStruct(halo_shape, F32),
            in_specs=[in_vmem] * 4,
            out_specs=in_vmem,
            scratch_shapes=[pltpu.VMEM(halo_shape, F32)] * 2 + [pltpu.SemaphoreType.DMA((2,))] * 2,
            compiler_params=pltpu.CompilerParams(collective_id=1, has_side_effects=True),
        )(density, momentum, tracer, cotangent)
        biases = [b.reshape(1, -1) for b in (b_in, b_mid, b_out)]
        weights = (w_in, biases[0], w_mid, biases[1], w_out, biases[2])
        extra = own + 32
        lines = own + 32
        out = pl.pallas_call(
            kernel,
            out_shape=(
                jax.ShapeDtypeStruct(density.shape, F32),
                jax.ShapeDtypeStruct(momentum.shape, F32),
                jax.ShapeDtypeStruct(tracer.shape, F32),
                jax.ShapeDtypeStruct((48, 128), F32),
            ),
            in_specs=[pl.BlockSpec(memory_space=pltpu.VMEM)] * 11,
            out_specs=tuple([pl.BlockSpec(memory_space=pltpu.VMEM)] * 4),
            scratch_shapes=[
                pltpu.VMEM((4, lines, width), F32),
                pltpu.VMEM((4, 2, extra, 128), F32),
                pltpu.VMEM((4, 2, extra, 128), F32),
                pltpu.VMEM((4 * extra, width), BF16),
                pltpu.VMEM((4 * extra, width), BF16),
                pltpu.VMEM((4 * extra, width), BF16),
                pltpu.VMEM((32 * lines, width), BF16),
                pltpu.VMEM((32 * lines, width), BF16),
                pltpu.VMEM((32 * lines, width), BF16),
                pltpu.VMEM((32 * lines, width), BF16),
                pltpu.VMEM((16 * lines, width), BF16),
                pltpu.VMEM((16 * lines, width), BF16),
                pltpu.VMEM((8, lines, width), F32),
                pltpu.VMEM((16, 2, extra, 128), F32),
                pltpu.VMEM((2, 4 * extra, 128), F32),
                pltpu.VMEM((4, own, width), F32),
                pltpu.VMEM((2, 128, 128), F32),
                pltpu.VMEM((2, 64, 128), F32),
                pltpu.VMEM((2, 64, 128), F32),
                pltpu.VMEM((2, 64, 128), F32),
                pltpu.VMEM((2, 64, 128), F32),
                pltpu.VMEM((2, 32, 128), F32),
                pltpu.VMEM((2, 128, 128), F32),
                pltpu.VMEM((48, 64), F32),
                pltpu.VMEM((80, 256), F32),
                pltpu.VMEM((64, 80), F32),
                pltpu.VMEM((32, 144), F32),
                pltpu.VMEM((64, 80), F32),
                pltpu.VMEM((32, 144), F32),
                pltpu.VMEM((32, 112), BF16),
                pltpu.VMEM((128, 208), BF16),
                pltpu.VMEM((32, 208), BF16),
                pltpu.VMEM((8, 208), BF16),
                pltpu.VMEM((64, 48), BF16),
                pltpu.VMEM((64, 192), BF16),
                pltpu.VMEM((16, 96), BF16),
                pltpu.VMEM((32, 384), BF16),
            ],
            compiler_params=pltpu.CompilerParams(vmem_limit_bytes=60 * 1024 * 1024),
        )(density, momentum, tracer, cotangent, halo, *weights)
        shape = (48, 128)
        total = pl.pallas_call(
            functools.partial(reduce_kernel, sizes),
            out_shape=jax.ShapeDtypeStruct(shape, F32),
            in_specs=[in_vmem],
            out_specs=in_vmem,
            scratch_shapes=[pltpu.VMEM((n,) + shape, F32) for n in sizes]
            + [pltpu.SemaphoreType.DMA((n,)) for n in sizes] * 2,
            compiler_params=pltpu.CompilerParams(collective_id=0, has_side_effects=True),
        )(out[3])
        totals = pl.pallas_call(
            unpack_kernel,
            out_shape=tuple(jax.ShapeDtypeStruct(w.shape, F32) for w in weights),
            in_specs=[in_vmem],
            out_specs=tuple([in_vmem] * 6),
        )(total)
        return (
            out[0],
            out[1],
            out[2],
            totals[0],
            totals[1].reshape(-1),
            totals[2],
            totals[3].reshape(-1),
            totals[4],
            totals[5].reshape(-1),
        )

    return body


def solution(mesh):
    in_specs = (
        P("traj", None, ("tx", "ty")),
        P("traj", None, None, ("tx", "ty")),
        P("traj", None, ("tx", "ty")),
        P("traj", None, None, ("tx", "ty")),
        P(), P(), P(), P(), P(), P(),
    )
    out_specs = (
        P("traj", None, ("tx", "ty")),
        P("traj", None, None, ("tx", "ty")),
        P("traj", None, ("tx", "ty")),
        P(), P(), P(), P(), P(), P(),
    )
    return jax.shard_map(
        make_body(ring_size(mesh), mesh.shape["ty"], tuple(mesh.shape[axis] for axis in GROUPS)), mesh=mesh, in_specs=in_specs, out_specs=out_specs, check_vma=False
    )
```

```python
import functools

import jax
import jax.numpy as jnp
from jax import lax
from jax.experimental import pallas as pl
from jax.experimental.pallas import tpu as pltpu
from jax.sharding import PartitionSpec as P

F32 = jnp.float32
BF16 = jnp.bfloat16
courant = 0.1
slope_gain = 0.25
HALO = 4
Y_ORDER = (0, 2, 1, 3)
STAGES = "bybybybyfbyfyfyfy"


def split(x):
    hi = x.astype(BF16)
    return hi, (x - hi.astype(F32)).astype(BF16)


def split3(x):
    hi = x.astype(BF16)
    rest = x - hi.astype(F32)
    mid = rest.astype(BF16)
    return hi, mid, (rest - mid.astype(F32)).astype(BF16)


def six(parts, ones):
    hi, mid, low = parts
    return rows(hi, mid, low, hi, mid, hi, ones)


def dot(a, b):
    return lax.dot_general(a, b, (((1,), (0,)), ((), ())), preferred_element_type=F32)


def dot_nt(a, b):
    return lax.dot_general(a, b, (((1,), (1,)), ((), ())), preferred_element_type=F32)


def exact(a, b, nt=False):
    dims = (((1,), (1 if nt else 0,)), ((), ()))
    return lax.dot_general(a, b, dims, preferred_element_type=F32, precision=lax.Precision.HIGHEST)


def rows(*parts):
    return jnp.concatenate(parts, 0)


def lanes(*parts):
    return jnp.concatenate(parts, 1)


def roll(v, amount):
    return pltpu.roll(v, amount % v.shape[1], 1)


def halves_at(lead, at):
    return [tuple(lead) + (t, at, slice(None)) for t in range(2)]


def get(ref, lead, at):
    return lanes(*[ref[where] for where in halves_at(lead, at)])


def put(ref, lead, at, value):
    for t, where in enumerate(halves_at(lead, at)):
        ref[where] = value[:, 128 * t : 128 * t + 128]


def face_states(cells, gates):
    below, here, above, above2 = cells
    slope_left = [above[c] - below[c] for c in range(4)]
    slope_right = [above2[c] - here[c] for c in range(4)]
    left = [here[c] + slope_gain * gates[c] * slope_left[c] for c in range(4)]
    right = [above[c] - slope_gain * gates[4 + c] * slope_right[c] for c in range(4)]
    return slope_left, slope_right, left, right


def flux_of(left, right):
    u_left = left[1] * (1.0 / left[0])
    u_right = right[1] * (1.0 / right[0])
    speed = 0.5 * jnp.maximum(jnp.abs(u_left), jnp.abs(u_right)) + 0.5
    physical = (
        left[1] + right[1],
        left[1] * u_left + left[0] + (right[1] * u_right + right[0]),
        left[2] * u_left + right[2] * u_right,
        left[3] * u_left + right[3] * u_right,
    )
    return [0.5 * physical[c] - speed * (right[c] - left[c]) for c in range(4)]


def flux_back(cells, gates, cot):
    slope_left, slope_right, left, right = face_states(cells, gates)
    inv_left = 1.0 / left[0]
    inv_right = 1.0 / right[0]
    u_left = left[1] * inv_left
    u_right = right[1] * inv_right
    abs_left = jnp.abs(u_left)
    abs_right = jnp.abs(u_right)
    half = [0.5 * v for v in cot]
    speed = jnp.maximum(abs_left, abs_right) + 1.0
    d_speed = half[0] * (left[0] - right[0])
    for c in range(1, 4):
        d_speed = d_speed + half[c] * (left[c] - right[c])
    share_left = jnp.where(abs_left > abs_right, 1.0, jnp.where(abs_left < abs_right, 0.0, 0.5))
    d_abs_left = d_speed * share_left
    d_abs_right = d_speed - d_abs_left

    def one_side(state, inv, u, d_abs, sign):
        signed = jnp.where(u > 0.0, d_abs, jnp.where(u < 0.0, -d_abs, 0.0))
        d_u = half[1] * state[1] + half[2] * state[2] + half[3] * state[3] + signed
        d_u = d_u * inv
        visc = [sign * (speed * half[c]) for c in range(4)]
        return (
            half[1] - d_u * u + visc[0],
            half[0] + half[1] * u + d_u + visc[1],
            half[2] * u + visc[2],
            half[3] * u + visc[3],
        )

    d_left = one_side(left, inv_left, u_left, d_abs_left, 1.0)
    d_right = one_side(right, inv_right, u_right, d_abs_right, -1.0)
    scaled_left = [slope_gain * v for v in d_left]
    scaled_right = [slope_gain * v for v in d_right]
    d_gates = [scaled_left[c] * slope_left[c] for c in range(4)]
    d_gates += [-(scaled_right[c] * slope_right[c]) for c in range(4)]
    minus_below = [gates[c] * scaled_left[c] for c in range(4)]
    minus_above2 = [gates[4 + c] * scaled_right[c] for c in range(4)]
    to_here = [d_left[c] + minus_above2[c] for c in range(4)]
    to_above = [d_right[c] + minus_below[c] for c in range(4)]
    return d_gates, minus_below, to_here, to_above, minus_above2


def index(shape, axis):
    return lax.broadcasted_iota(jnp.int32, shape, axis)


def indicator(condition, dtype=F32):
    return jnp.where(condition, 1.0, 0.0).astype(F32).astype(dtype)


def fill_weights(given, filled):
    w_in_t, b_in, w_mid, b_mid, w_out, b_out = [ref[...] for ref in given]
    w_in = w_in_t.T
    w_x, w_y, w_m, w_o, w_ot, w_mt, w_xt, w_yt = filled

    def bias_columns(bias, count, depth):
        parts = split3(jnp.broadcast_to(bias, (16, count)))
        r = index((16, count), 0)
        stacked = jnp.zeros((16, count), F32)
        for at in range(3):
            stacked = jnp.where(r == at, parts[at].astype(F32), stacked)
        below = jnp.zeros((depth, count), BF16)
        unit = indicator(index((count, count), 0) == index((count, count), 1), BF16)
        return dot_nt(unit, rows(below, stacked.astype(BF16)))

    def spread(parts, owners, block, columns, offset=0):
        count = parts[0].shape[1]
        r, k = index((count, columns), 0), index((count, columns), 1)
        total = None
        for at, part in enumerate(parts):
            inside = jnp.logical_and(k >= owners[at][0] * block, k < owners[at][1] * block)
            where = jnp.logical_and(inside, k % block == r + offset)
            piece = dot(part, indicator(where, BF16))
            total = piece if total is None else total + piece
        return total

    sixfold = ((0, 3), (3, 5), (5, 6))
    threefold = ((0, 2), (2, 3))
    for ref, weight, bias in ((w_x, w_in, b_in), (w_m, w_mid, b_mid)):
        units, count = weight.shape
        value = spread(split3(weight), sixfold, count, 6 * count + 16)
        ref[...] = (value + bias_columns(bias, units, 6 * count)).astype(BF16)
    out_parts = split3(w_out)
    for at, part in enumerate(out_parts):
        value = spread([part], ((0, 3 - at),), 32, 112)
        if at == 0:
            value = value + bias_columns(b_out, 8, 96)
        w_o[8 * at : 8 * at + 8, :] = value
    in_parts = split3(w_in)
    in_bias = bias_columns(b_in, 32, 192)
    for face in range(4):
        value = spread(in_parts, sixfold, 32, 208, 4 * face) + in_bias
        w_y[32 * face : 32 * face + 32, :] = value.astype(BF16)

    def turned(weight, lines):
        units = weight.shape[1]
        r, k = index((lines * units, units), 0), index((lines * units, units), 1)
        chosen = indicator(r % units == k, BF16)
        return [dot_nt(chosen, part).astype(BF16) for part in split(weight)]

    for ref, weight in ((w_ot, w_out), (w_mt, w_mid)):
        gates, units = weight.shape
        parts = turned(weight, 2)
        shape = (2 * units, 6 * gates)
        r, k = index(shape, 0), index(shape, 1)
        value = spread(parts, ((0, 4), (4, 6)), gates, 6 * gates)
        ref[...] = jnp.where((k // gates) % 2 == r // units, value, 0.0).astype(BF16)
    w_xt[...] = spread(turned(w_in, 1), threefold, 32, 96).astype(BF16)
    total = None
    for face in range(4):
        r, k = index((32, 16), 0), index((32, 16), 1)
        chosen = indicator(r == k + 4 * face, BF16)
        parts = [dot_nt(chosen, part).astype(BF16) for part in split(w_in)]
        value = spread(parts, threefold, 128, 384, 32 * face)
        total = value if total is None else total + value
    w_yt[...] = total.astype(BF16)


def kernel(
    density, momentum, tracer, cotangent, halo,
    w_in, b_in, w_mid, b_mid, w_out, b_out,
    g_density, g_momentum, g_tracer, packed,
    nat, cot, mid, mid_hi, mid_lo, mid_lo2,
    h1_hi, h1_lo, h2_hi, h2_lo, t_hi, t_lo, gate_x,
    face, d_mix, out_nat,
    xi, gi, gi_y, di, di_y, mi, zi,
    acc_x, acc_y, acc_m, acc_o, acc_my, acc_oy,
    w_x, w_y, w_m, w_o, w_ot, w_mt, w_xt, w_yt,
):
    width = nat.shape[2]
    own = density.shape[2]
    blocks = own // 8
    ones = jnp.ones((16, width), BF16)
    fill_weights(
        (w_in, b_in, w_mid, b_mid, w_out, b_out), (w_x, w_y, w_m, w_o, w_ot, w_mt, w_xt, w_yt)
    )

    for c in range(4):
        if c == 0:
            source = density[0]
        elif c == 3:
            source = tracer[0]
        else:
            source = momentum[0, c - 1]
        nat[c, 8 : 8 + own, :] = source.T
        for side in range(2):
            edge = halo[side, 4 * c : 4 * c + 4, :]
            nat[c, 4 * side : 4 * side + 4, :] = edge
            nat[c, 8 + own + 4 * side : 12 + own + 4 * side, :] = edge
        put(cot, (c,), pl.ds(8, own), cotangent[0, c].T)
        for side in range(2):
            edge = halo[side, 16 + 4 * c : 20 + 4 * c, :]
            put(cot, (c,), pl.ds(4 * side, 4), edge)
            put(cot, (c,), pl.ds(8 + own + 4 * side, 4), edge)
    acc_x[...] = jnp.zeros_like(acc_x)
    acc_y[...] = jnp.zeros_like(acc_y)
    acc_m[...] = jnp.zeros_like(acc_m)
    acc_o[...] = jnp.zeros_like(acc_o)
    acc_my[...] = jnp.zeros_like(acc_my)
    acc_oy[...] = jnp.zeros_like(acc_oy)

    def middle(pre):
        firsts = [split3(jnp.tanh(v)) for v in pre]
        return firsts, [dot(w_m[...], six(v, ones)) for v in firsts]

    def output(pre):
        seconds = [split3(jnp.tanh(v)) for v in pre]
        weight = w_o[...].astype(BF16)
        nexts = []
        for v in seconds:
            three = dot(weight, rows(*v, ones))
            nexts.append(three[0:8] + (three[8:16] + three[16:24]))
        return seconds, nexts

    def natural_gates(pre, gi):
        for line in range(8):
            put(gi, (), pl.ds(8 * line, 8), jnp.tanh(pre[line]))
        return [get(gi, (), pl.ds(g, 8, stride=8)) for g in range(8)]

    def back_output(gates, d_gates, di, load_second):
        for g in range(8):
            put(di, (), pl.ds(g, 8, stride=8), d_gates[g] * (1.0 - gates[g] * gates[g]))
        outs, pres = [], []
        for pair in range(4):
            o_hi, o_lo = split(get(di, (), pl.ds(16 * pair, 16)))
            outs.append((o_hi, o_lo))
            pres.append(dot(w_ot[...], rows(o_hi, o_lo, o_hi)))
        return outs, pres

    def back_through(pres, load, weight):
        parts, nexts = [], []
        for pair in range(4):
            s_hi, s_lo = load(pair)
            value = s_hi.astype(F32) + s_lo.astype(F32)
            part = split(pres[pair] * (1.0 - value * value))
            parts.append(part)
            if weight is not None:
                nexts.append(dot(weight[...], rows(part[0], part[1], part[0])))
        return parts, nexts

    def weight_sums(outs, d_second, load_first, load_second, acc_m, acc_o, valid):
        mid_lhs, mid_rhs, out_lhs, out_rhs = [], [], [], []
        for pair in range(4):
            f_hi, f_lo = load_first(pair)
            for line in range(2):
                at = slice(32 * line, 32 * line + 32)
                mid_lhs.append(rows(d_second[pair][0][at], d_second[pair][1][at]))
                mid_rhs.append(rows(f_hi[at], f_lo[at], ones))
            out_lhs.append(rows(*outs[pair]))
            out_rhs.append(rows(*load_second(pair), ones))
        acc_m[...] += jnp.where(valid, dot_nt(lanes(*mid_lhs), lanes(*mid_rhs)), 0.0)
        acc_o[...] += jnp.where(valid, dot_nt(lanes(*out_lhs), lanes(*out_rhs)), 0.0)

    def x_forward(b):
        n0 = pl.multiple_of(8 * b, 8)
        here = [nat[c, pl.ds(n0, 8), :] for c in range(4)]
        cells = [[roll(v, 1) for v in here], here, [roll(v, -1) for v in here], [roll(v, -2) for v in here]]
        for s in range(4):
            for c in range(4):
                put(xi, (), pl.ds(4 * s + c, 8, stride=16), cells[s][c])
        pre = []
        for line in range(8):
            window = split3(get(xi, (), pl.ds(16 * line, 16)))
            at = pl.ds(pl.multiple_of(128 * b + 16 * line, 16), 16)
            t_hi[at, :] = window[0]
            t_lo[at, :] = window[1]
            pre.append(dot(w_x[...], six(window, ones)))
        yield
        firsts, pre = middle(pre)
        for line in range(8):
            at = pl.ds(pl.multiple_of(256 * b + 32 * line, 32), 32)
            h1_hi[at, :] = firsts[line][0]
            h1_lo[at, :] = firsts[line][1]
        yield
        seconds, pre = output(pre)
        for line in range(8):
            at = pl.ds(pl.multiple_of(256 * b + 32 * line, 32), 32)
            h2_hi[at, :] = seconds[line][0]
            h2_lo[at, :] = seconds[line][1]
        yield
        gates = natural_gates(pre, gi)
        for g in range(8):
            gate_x[g, pl.ds(n0, 8), :] = gates[g]
        _, _, left, right = face_states(cells, gates)
        fluxes = flux_of(left, right)
        for c in range(4):
            value = here[c] - courant * (fluxes[c] - roll(fluxes[c], 1))
            put(mid, (c,), pl.ds(n0, 8), value)
            put(mi, (), pl.ds(Y_ORDER[c], 8, stride=4), value)
        at = pl.ds(pl.multiple_of(32 * b, 32), 32)
        for ref, part in zip((mid_hi, mid_lo, mid_lo2), split3(get(mi, (), pl.ds(0, 32)))):
            ref[at, :] = part
        yield

    d_mix[:, 0:16, :] = jnp.zeros((2, 16, 128), F32)

    def y_sweep(b, valid):
        n0 = pl.multiple_of(8 * b, 8)
        windows, pre = [], []
        for q in range(2):
            at = pl.ds(pl.multiple_of(32 * b + 16 * q, 16), 32)
            window = mid_hi[at, :], mid_lo[at, :], mid_lo2[at, :]
            windows.append(rows(window[0], window[1], ones))
            four = dot(w_y[...], six(window, ones))
            pre += [four[32 * line : 32 * line + 32] for line in range(4)]
        yield
        firsts, pre = middle(pre)
        yield
        seconds, pre = output(pre)
        yield
        gates = natural_gates(pre, gi_y)
        cells = [[get(mid, (c,), pl.ds(n0 + k, 8)) for c in Y_ORDER] for k in range(4)]
        cots = [courant * (get(cot, (c,), pl.ds(n0 + 2, 8)) - get(cot, (c,), pl.ds(n0 + 1, 8))) for c in Y_ORDER]
        d_gates, minus_below, to_here, to_above, minus_above2 = flux_back(cells, gates, cots)
        for c in range(4):
            to = Y_ORDER[c]
            put(face, (to,), pl.ds(n0, 8), minus_below[c])
            put(face, (4 + to,), pl.ds(n0, 8), to_here[c])
            put(face, (8 + to,), pl.ds(n0, 8), to_above[c])
            put(face, (12 + to,), pl.ds(n0, 8), minus_above2[c])

        def load(parts):
            return lambda pair: [rows(parts[2 * pair][k], parts[2 * pair + 1][k]) for k in range(2)]

        outs, pres = back_output(gates, d_gates, di_y, load(seconds))
        yield
        d_second, pres = back_through(pres, load(seconds), w_mt)
        yield
        d_first, _ = back_through(pres, load(firsts), None)
        combined, right_side = [], []
        for q in range(2):
            hi = rows(d_first[2 * q][0], d_first[2 * q + 1][0])
            lo = rows(d_first[2 * q][1], d_first[2 * q + 1][1])
            combined.append(dot(w_yt[...], rows(hi, lo, hi)))
            right_side.append(rows(hi, lo))
        yield
        weight_sums(outs, d_second, load(firsts), load(seconds), acc_my, acc_oy, valid)
        yield
        acc_y[...] += jnp.where(valid, dot_nt(lanes(*windows), lanes(*right_side)), 0.0)
        at = pl.multiple_of(32 * b, 32)
        put(d_mix, (), pl.ds(at, 16), get(d_mix, (), pl.ds(at, 16)) + combined[0][:16])
        put(d_mix, (), pl.ds(at + 16, 16), combined[0][16:] + combined[1][:16])
        put(d_mix, (), pl.ds(at + 32, 16), combined[1][16:])
        yield

    def x_back(b, valid):
        n0 = pl.multiple_of(8 * b, 8)
        gates = [gate_x[g, pl.ds(n0, 8), :] for g in range(8)]
        here = [nat[c, pl.ds(n0, 8), :] for c in range(4)]
        cells = [[roll(v, 1) for v in here], here, [roll(v, -1) for v in here], [roll(v, -2) for v in here]]
        back = []
        for c in range(4):
            value = get(cot, (c,), pl.ds(n0, 8)) + get(d_mix, (), pl.ds(4 * n0 + Y_ORDER[c], 8, stride=4))
            value = value + get(face, (4 + c,), pl.ds(n0 - 1, 8)) - get(face, (c,), pl.ds(n0, 8))
            value = value + get(face, (8 + c,), pl.ds(n0 - 2, 8)) - get(face, (12 + c,), pl.ds(n0 - 3, 8))
            back.append(value)
        cots = [courant * (roll(v, -1) - v) for v in back]
        d_gates, minus_below, to_here, to_above, minus_above2 = flux_back(cells, gates, cots)

        def load(hi_ref, lo_ref):
            def of(pair):
                at = pl.ds(pl.multiple_of(256 * b + 64 * pair, 64), 64)
                return hi_ref[at, :], lo_ref[at, :]
            return of

        first, second = load(h1_hi, h1_lo), load(h2_hi, h2_lo)
        outs, pres = back_output(gates, d_gates, di, second)
        direct = [
            (back[c] + to_here[c], minus_below[c], to_above[c], minus_above2[c]) for c in range(4)
        ]
        yield
        d_second, pres = back_through(pres, second, w_mt)
        yield
        d_first, _ = back_through(pres, first, None)
        left_side, right_side = [], []
        for line in range(8):
            at = pl.ds(pl.multiple_of(128 * b + 16 * line, 16), 16)
            left_side.append(rows(t_hi[at, :], t_lo[at, :], ones))
            at = slice(32 * (line % 2), 32 * (line % 2) + 32)
            hi, lo = [v[at] for v in d_first[line // 2]]
            right_side.append(rows(hi, lo))
            put(zi, (), pl.ds(16 * line, 16), dot(w_xt[...], rows(hi, lo, hi)))
        yield
        weight_sums(outs, d_second, first, second, acc_m, acc_o, valid)
        acc_x[...] += jnp.where(valid, dot_nt(lanes(*left_side), lanes(*right_side)), 0.0)
        yield
        for c in range(4):
            parts = [get(zi, (), pl.ds(4 * s + c, 8, stride=16)) for s in range(4)]
            value = direct[c][0] + parts[1] + roll(parts[0] - direct[c][1], -1)
            value = value + roll(direct[c][2] + parts[2], 1) + roll(parts[3] - direct[c][3], 2)
            out_nat[c, pl.ds(pl.multiple_of(n0 - 8, 8), 8), :] = value
        yield

    def step(i, carry):
        back = x_back(jnp.maximum(i - 3, 1), i >= 4)
        sweep = y_sweep(jnp.maximum(i - 2, 0), jnp.logical_and(i >= 3, i <= blocks + 2))
        ahead = x_forward(i)
        for stage in STAGES:
            next({"b": back, "y": sweep, "f": ahead}[stage])
        return carry

    lax.fori_loop(0, blocks + 4, step, 0)

    g_density[0] = out_nat[0].T
    g_momentum[0, 0] = out_nat[1].T
    g_momentum[0, 1] = out_nat[2].T
    g_tracer[0] = out_nat[3].T

    acc_m[...] += acc_my[...]
    acc_o[...] += acc_oy[...]
    r, k = index((24, 48), 0), index((24, 48), 1)
    pick = jnp.where(k < 32, k % 16, jnp.where(k == 32, 16, -1))
    first_x = exact(indicator(r == pick), acc_x[...])
    r, k = index((80, 256), 0), index((80, 256), 1)
    distance = (r // 4) % 8 - (k // 32) % 4
    rr, kk = index((24, 80), 0), index((24, 80), 1)
    masked = jnp.where(r == 64, acc_y[...], 0.0)
    first_y = exact(indicator(jnp.logical_and(rr == 16, kk == 64)), masked)
    for s in range(4):
        masked = jnp.where(jnp.logical_and(r < 64, distance == s), acc_y[...], 0.0)
        first_y = first_y + exact(indicator(jnp.logical_and(rr == 4 * s + kk % 4, kk < 64)), masked)

    def by_unit(shape, axis):
        return indicator(index(shape, axis) % 32 == index(shape, 1 - axis))

    first = exact(by_unit((32, 64), 1), first_x, nt=True) + exact(by_unit((32, 256), 1), first_y, nt=True)
    first_bias = exact(first_x, by_unit((64, 32), 0)) + exact(first_y, by_unit((256, 32), 0))
    r, k = index((24, 128), 0), index((24, 128), 1)
    total = exact(first, indicator(jnp.logical_and(k == r + 64, r < 16)))
    r, k = index((80, 128), 0), index((80, 128), 1)
    total = total + exact(exact(by_unit((32, 64), 1), acc_m[...]), indicator(jnp.logical_and(r % 32 == k, r < 64)))
    second_bias = exact(exact(indicator(index((8, 80), 1) == 64), acc_m[...], nt=True), by_unit((64, 32), 0))
    r, k = index((32, 144), 0), index((32, 144), 1)
    masked = jnp.where(jnp.logical_and(k < 128, (r // 8) % 2 == (k // 32) % 2), acc_o[...], 0.0)
    r, k = index((8, 32), 0), index((8, 32), 1)
    summed = exact(indicator(r == k % 8), masked)
    r, k = index((144, 128), 0), index((144, 128), 1)
    packed[0:8, :] = total[0:8] + exact(summed, indicator(jnp.logical_and(r % 32 + 96 == k, r < 128)))
    packed[16:32, :] = total[16:32]
    out_bias = exact(indicator(index((8, 144), 1) == 128), acc_o[...], nt=True)
    r, k = index((32, 128), 0), index((32, 128), 1)
    out_bias = exact(out_bias, indicator(r % 8 + 96 == k))
    r, k = index((32, 128), 0), index((32, 128), 1)
    wide = indicator(r + 96 == k)
    first_bias = exact(first_bias[16:24], wide)
    second_bias = exact(second_bias, wide)
    r = index((8, 128), 0)
    first_bias = jnp.broadcast_to(first_bias[0:1], (8, 128))
    packed[8:16, :] = total[8:16] + jnp.where(
        r == 0, first_bias, jnp.where(r == 1, second_bias, jnp.where(r == 2, out_bias, 0.0))
    )


def halo_kernel(size, inner, density, momentum, tracer, cotangent, halo, sent, landed, send_sem, recv_sem):
    mesh_ids = pl.DeviceIdType.MESH
    here = lax.axis_index("tx") * inner + lax.axis_index("ty")
    peers = []
    for step in (size - 1, 1):
        peer = lax.rem(here + step, size)
        peers.append({"tx": peer // inner, "ty": lax.rem(peer, inner)})
    barrier = pltpu.get_barrier_semaphore()
    for peer in peers:
        pl.semaphore_signal(barrier, inc=1, device_id=peer, device_id_type=mesh_ids)
    own = density.shape[2]
    for c in range(8):
        if c >= 4:
            source = cotangent[0, c - 4]
        elif c == 0:
            source = density[0]
        elif c == 3:
            source = tracer[0]
        else:
            source = momentum[0, c - 1]
        lines = source.T
        sent[0, 4 * c : 4 * c + 4, :] = lines[:HALO]
        sent[1, 4 * c : 4 * c + 4, :] = lines[own - HALO :]
    pl.semaphore_wait(barrier, 2)
    copies = [
        pltpu.make_async_remote_copy(
            src_ref=sent.at[side],
            dst_ref=landed.at[side],
            send_sem=send_sem.at[side],
            recv_sem=recv_sem.at[side],
            device_id=peers[side],
            device_id_type=mesh_ids,
        )
        for side in range(2)
    ]
    for copy in copies:
        copy.start()
    for copy in copies:
        copy.wait()
    halo[...] = landed[...]


GROUPS = ("traj", "ty", "tx")


def reduce_kernel(sizes, mine, total, *scratch):
    count = len(sizes)
    slots, sends, receives = scratch[:count], scratch[count : 2 * count], scratch[2 * count :]
    mesh_ids = pl.DeviceIdType.MESH
    barrier = pltpu.get_barrier_semaphore()
    for axis, size in zip(GROUPS, sizes):
        here = lax.axis_index(axis)
        for step in range(1, size):
            peer = lax.rem(here + step, size)
            pl.semaphore_signal(barrier, inc=1, device_id={axis: peer}, device_id_type=mesh_ids)
    pl.semaphore_wait(barrier, sum(sizes) - count)
    value = mine[...]
    for at, (axis, size) in enumerate(zip(GROUPS, sizes)):
        here = lax.axis_index(axis)
        slots[at][here] = value
        copies = []
        for step in range(1, size):
            peer = lax.rem(here + step, size)
            copies.append(
                pltpu.make_async_remote_copy(
                    src_ref=slots[at].at[here],
                    dst_ref=slots[at].at[here],
                    send_sem=sends[at].at[step],
                    recv_sem=receives[at].at[step],
                    device_id={axis: peer},
                    device_id_type=mesh_ids,
                )
            )
        for copy in copies:
            copy.start()
        for copy in copies:
            copy.wait()
        value = slots[at][0]
        for other in range(1, size):
            value = value + slots[at][other]
    total[...] = value


def unpack_kernel(total, g_w_in, g_b_in, g_w_mid, g_b_mid, g_w_out, g_b_out):
    g_w_in[...] = total[0:32, :].T[64:80]
    g_b_in[...] = total[8:9, 96:128]
    g_w_mid[...] = total[0:32, 0:32]
    g_b_mid[...] = total[9:10, 96:128]
    g_w_out[...] = total[0:8, 96:128]
    g_b_out[...] = total[10:11, 96:104]


def ring_size(mesh):
    return mesh.shape["tx"] * mesh.shape["ty"]


def make_body(size, inner, sizes):
    def body(density, momentum, tracer, cotangent, w_in, b_in, w_mid, b_mid, w_out, b_out):
        own, width = density.shape[2], density.shape[1]
        in_vmem = pl.BlockSpec(memory_space=pltpu.VMEM)
        halo_shape = (2, 8 * HALO, width)
        halo = pl.pallas_call(
            functools.partial(halo_kernel, size, inner),
            out_shape=jax.ShapeDtypeStruct(halo_shape, F32),
            in_specs=[in_vmem] * 4,
            out_specs=in_vmem,
            scratch_shapes=[pltpu.VMEM(halo_shape, F32)] * 2 + [pltpu.SemaphoreType.DMA((2,))] * 2,
            compiler_params=pltpu.CompilerParams(collective_id=1, has_side_effects=True),
        )(density, momentum, tracer, cotangent)
        biases = [b.reshape(1, -1) for b in (b_in, b_mid, b_out)]
        weights = (w_in.T, biases[0], w_mid, biases[1], w_out, biases[2])
        extra = own + 32
        lines = own + 32
        out = pl.pallas_call(
            kernel,
            out_shape=(
                jax.ShapeDtypeStruct(density.shape, F32),
                jax.ShapeDtypeStruct(momentum.shape, F32),
                jax.ShapeDtypeStruct(tracer.shape, F32),
                jax.ShapeDtypeStruct((32, 128), F32),
            ),
            in_specs=[pl.BlockSpec(memory_space=pltpu.VMEM)] * 11,
            out_specs=tuple([pl.BlockSpec(memory_space=pltpu.VMEM)] * 4),
            scratch_shapes=[
                pltpu.VMEM((4, lines, width), F32),
                pltpu.VMEM((4, 2, extra, 128), F32),
                pltpu.VMEM((4, 2, extra, 128), F32),
                pltpu.VMEM((4 * extra, width), BF16),
                pltpu.VMEM((4 * extra, width), BF16),
                pltpu.VMEM((4 * extra, width), BF16),
                pltpu.VMEM((32 * lines, width), BF16),
                pltpu.VMEM((32 * lines, width), BF16),
                pltpu.VMEM((32 * lines, width), BF16),
                pltpu.VMEM((32 * lines, width), BF16),
                pltpu.VMEM((16 * lines, width), BF16),
                pltpu.VMEM((16 * lines, width), BF16),
                pltpu.VMEM((8, lines, width), F32),
                pltpu.VMEM((16, 2, extra, 128), F32),
                pltpu.VMEM((2, 4 * extra, 128), F32),
                pltpu.VMEM((4, own, width), F32),
                pltpu.VMEM((2, 128, 128), F32),
                pltpu.VMEM((2, 64, 128), F32),
                pltpu.VMEM((2, 64, 128), F32),
                pltpu.VMEM((2, 64, 128), F32),
                pltpu.VMEM((2, 64, 128), F32),
                pltpu.VMEM((2, 32, 128), F32),
                pltpu.VMEM((2, 128, 128), F32),
                pltpu.VMEM((48, 64), F32),
                pltpu.VMEM((80, 256), F32),
                pltpu.VMEM((64, 80), F32),
                pltpu.VMEM((32, 144), F32),
                pltpu.VMEM((64, 80), F32),
                pltpu.VMEM((32, 144), F32),
                pltpu.VMEM((32, 112), BF16),
                pltpu.VMEM((128, 208), BF16),
                pltpu.VMEM((32, 208), BF16),
                pltpu.VMEM((24, 112), F32),
                pltpu.VMEM((64, 48), BF16),
                pltpu.VMEM((64, 192), BF16),
                pltpu.VMEM((16, 96), BF16),
                pltpu.VMEM((32, 384), BF16),
            ],
            compiler_params=pltpu.CompilerParams(vmem_limit_bytes=60 * 1024 * 1024),
        )(density, momentum, tracer, cotangent, halo, *weights)
        shape = (32, 128)
        total = pl.pallas_call(
            functools.partial(reduce_kernel, sizes),
            out_shape=jax.ShapeDtypeStruct(shape, F32),
            in_specs=[in_vmem],
            out_specs=in_vmem,
            scratch_shapes=[pltpu.VMEM((n,) + shape, F32) for n in sizes]
            + [pltpu.SemaphoreType.DMA((n,)) for n in sizes] * 2,
            compiler_params=pltpu.CompilerParams(collective_id=0, has_side_effects=True),
        )(out[3])
        totals = pl.pallas_call(
            unpack_kernel,
            out_shape=tuple(jax.ShapeDtypeStruct(w.shape, F32) for w in weights),
            in_specs=[in_vmem],
            out_specs=tuple([in_vmem] * 6),
        )(total)
        return (
            out[0],
            out[1],
            out[2],
            totals[0].T,
            totals[1].reshape(-1),
            totals[2],
            totals[3].reshape(-1),
            totals[4],
            totals[5].reshape(-1),
        )

    return body


def solution(mesh):
    in_specs = (
        P("traj", None, ("tx", "ty")),
        P("traj", None, None, ("tx", "ty")),
        P("traj", None, ("tx", "ty")),
        P("traj", None, None, ("tx", "ty")),
        P(), P(), P(), P(), P(), P(),
    )
    out_specs = (
        P("traj", None, ("tx", "ty")),
        P("traj", None, None, ("tx", "ty")),
        P("traj", None, ("tx", "ty")),
        P(), P(), P(), P(), P(), P(),
    )
    return jax.shard_map(
        make_body(ring_size(mesh), mesh.shape["ty"], tuple(mesh.shape[axis] for axis in GROUPS)), mesh=mesh, in_specs=in_specs, out_specs=out_specs, check_vma=False
    )
```

```python
import functools

import jax
import jax.numpy as jnp
from jax import lax
from jax.experimental import pallas as pl
from jax.experimental.pallas import tpu as pltpu
from jax.sharding import PartitionSpec as P

F32 = jnp.float32
BF16 = jnp.bfloat16
courant = 0.1
slope_gain = 0.25
HALO = 4
Y_ORDER = (0, 2, 1, 3)
STAGES = "bfybfybfybyfbyyyy"


def split(x):
    hi = x.astype(BF16)
    return hi, (x - hi.astype(F32)).astype(BF16)


def split3(x):
    hi = x.astype(BF16)
    rest = x - hi.astype(F32)
    mid = rest.astype(BF16)
    return hi, mid, (rest - mid.astype(F32)).astype(BF16)


def six(parts, ones):
    hi, mid, low = parts
    return rows(hi, mid, low, hi, mid, hi, ones)


def dot(a, b):
    return lax.dot_general(a, b, (((1,), (0,)), ((), ())), preferred_element_type=F32)


def dot_nt(a, b):
    return lax.dot_general(a, b, (((1,), (1,)), ((), ())), preferred_element_type=F32)


def exact(a, b, nt=False):
    dims = (((1,), (1 if nt else 0,)), ((), ()))
    return lax.dot_general(a, b, dims, preferred_element_type=F32, precision=lax.Precision.HIGHEST)


def rows(*parts):
    return jnp.concatenate(parts, 0)


def lanes(*parts):
    return jnp.concatenate(parts, 1)


def roll(v, amount):
    return pltpu.roll(v, amount % v.shape[1], 1)


def halves_at(lead, at):
    return [tuple(lead) + (t, at, slice(None)) for t in range(2)]


def get(ref, lead, at):
    return lanes(*[ref[where] for where in halves_at(lead, at)])


def put(ref, lead, at, value):
    for t, where in enumerate(halves_at(lead, at)):
        ref[where] = value[:, 128 * t : 128 * t + 128]


def face_states(cells, gates):
    below, here, above, above2 = cells
    slope_left = [above[c] - below[c] for c in range(4)]
    slope_right = [above2[c] - here[c] for c in range(4)]
    left = [here[c] + slope_gain * gates[c] * slope_left[c] for c in range(4)]
    right = [above[c] - slope_gain * gates[4 + c] * slope_right[c] for c in range(4)]
    return slope_left, slope_right, left, right


def flux_of(left, right):
    u_left = left[1] * (1.0 / left[0])
    u_right = right[1] * (1.0 / right[0])
    speed = 0.5 * jnp.maximum(jnp.abs(u_left), jnp.abs(u_right)) + 0.5
    physical = (
        left[1] + right[1],
        left[1] * u_left + left[0] + (right[1] * u_right + right[0]),
        left[2] * u_left + right[2] * u_right,
        left[3] * u_left + right[3] * u_right,
    )
    return [0.5 * physical[c] - speed * (right[c] - left[c]) for c in range(4)]


def flux_back(cells, gates, cot):
    slope_left, slope_right, left, right = face_states(cells, gates)
    inv_left = 1.0 / left[0]
    inv_right = 1.0 / right[0]
    u_left = left[1] * inv_left
    u_right = right[1] * inv_right
    abs_left = jnp.abs(u_left)
    abs_right = jnp.abs(u_right)
    half = [0.5 * v for v in cot]
    speed = jnp.maximum(abs_left, abs_right) + 1.0
    d_speed = half[0] * (left[0] - right[0])
    for c in range(1, 4):
        d_speed = d_speed + half[c] * (left[c] - right[c])
    share_left = jnp.where(abs_left > abs_right, 1.0, jnp.where(abs_left < abs_right, 0.0, 0.5))
    d_abs_left = d_speed * share_left
    d_abs_right = d_speed - d_abs_left

    def one_side(state, inv, u, d_abs, sign):
        signed = jnp.where(u > 0.0, d_abs, jnp.where(u < 0.0, -d_abs, 0.0))
        d_u = half[1] * state[1] + half[2] * state[2] + half[3] * state[3] + signed
        d_u = d_u * inv
        visc = [sign * (speed * half[c]) for c in range(4)]
        return (
            half[1] - d_u * u + visc[0],
            half[0] + half[1] * u + d_u + visc[1],
            half[2] * u + visc[2],
            half[3] * u + visc[3],
        )

    d_left = one_side(left, inv_left, u_left, d_abs_left, 1.0)
    d_right = one_side(right, inv_right, u_right, d_abs_right, -1.0)
    scaled_left = [slope_gain * v for v in d_left]
    scaled_right = [slope_gain * v for v in d_right]
    d_gates = [scaled_left[c] * slope_left[c] for c in range(4)]
    d_gates += [-(scaled_right[c] * slope_right[c]) for c in range(4)]
    minus_below = [gates[c] * scaled_left[c] for c in range(4)]
    minus_above2 = [gates[4 + c] * scaled_right[c] for c in range(4)]
    to_here = [d_left[c] + minus_above2[c] for c in range(4)]
    to_above = [d_right[c] + minus_below[c] for c in range(4)]
    return d_gates, minus_below, to_here, to_above, minus_above2


def index(shape, axis):
    return lax.broadcasted_iota(jnp.int32, shape, axis)


def indicator(condition, dtype=F32):
    return jnp.where(condition, 1.0, 0.0).astype(F32).astype(dtype)


def fill_weights(given, filled):
    w_in_t, b_in, w_mid, b_mid, w_out, b_out = [ref[...] for ref in given]
    w_in = w_in_t.T
    w_x, w_y, w_m, w_o, w_ot, w_mt, w_xt, w_yt = filled

    def bias_columns(bias, count, depth):
        parts = split3(jnp.broadcast_to(bias, (16, count)))
        r = index((16, count), 0)
        stacked = jnp.zeros((16, count), F32)
        for at in range(3):
            stacked = jnp.where(r == at, parts[at].astype(F32), stacked)
        below = jnp.zeros((depth, count), BF16)
        unit = indicator(index((count, count), 0) == index((count, count), 1), BF16)
        return dot_nt(unit, rows(below, stacked.astype(BF16)))

    def spread(parts, owners, block, columns, offset=0):
        count = parts[0].shape[1]
        r, k = index((count, columns), 0), index((count, columns), 1)
        total = None
        for at, part in enumerate(parts):
            inside = jnp.logical_and(k >= owners[at][0] * block, k < owners[at][1] * block)
            where = jnp.logical_and(inside, k % block == r + offset)
            piece = dot(part, indicator(where, BF16))
            total = piece if total is None else total + piece
        return total

    sixfold = ((0, 3), (3, 5), (5, 6))
    threefold = ((0, 2), (2, 3))
    for ref, weight, bias in ((w_x, w_in, b_in),):
        units, count = weight.shape
        value = spread(split3(weight), sixfold, count, 6 * count + 16)
        ref[...] = (value + bias_columns(bias, units, 6 * count)).astype(BF16)
    mid_parts = split3(w_mid)
    upper = spread(mid_parts[:1], ((0, 3),), 32, 144) + bias_columns(b_mid, 32, 128)
    lower = spread(mid_parts[1:], ((0, 2), (3, 4)), 32, 144)
    w_m[...] = rows(upper, lower).astype(BF16)
    out_parts = split3(w_out)
    for at, part in enumerate(out_parts):
        value = spread([part], ((0, 3 - at),), 32, 112)
        if at == 0:
            value = value + bias_columns(b_out, 8, 96)
        w_o[8 * at : 8 * at + 8, :] = value
    in_parts = split3(w_in)
    in_bias = bias_columns(b_in, 32, 192)
    for face in range(4):
        value = spread(in_parts, sixfold, 32, 208, 4 * face) + in_bias
        w_y[32 * face : 32 * face + 32, :] = value.astype(BF16)

    def turned(weight, lines):
        units = weight.shape[1]
        r, k = index((lines * units, units), 0), index((lines * units, units), 1)
        chosen = indicator(r % units == k, BF16)
        return [dot_nt(chosen, part).astype(BF16) for part in split(weight)]

    for ref, weight in ((w_ot, w_out), (w_mt, w_mid)):
        gates, units = weight.shape
        parts = turned(weight, 2)
        shape = (2 * units, 6 * gates)
        r, k = index(shape, 0), index(shape, 1)
        value = spread(parts, ((0, 4), (4, 6)), gates, 6 * gates)
        ref[...] = jnp.where((k // gates) % 2 == r // units, value, 0.0).astype(BF16)
    w_xt[...] = spread(turned(w_in, 1), threefold, 32, 96).astype(BF16)
    total = None
    for face in range(4):
        r, k = index((32, 16), 0), index((32, 16), 1)
        chosen = indicator(r == k + 4 * face, BF16)
        parts = [dot_nt(chosen, part).astype(BF16) for part in split(w_in)]
        value = spread(parts, threefold, 128, 384, 32 * face)
        total = value if total is None else total + value
    w_yt[...] = total.astype(BF16)


def kernel(
    density, momentum, tracer, cotangent, halo,
    w_in, b_in, w_mid, b_mid, w_out, b_out,
    g_density, g_momentum, g_tracer, packed,
    nat, cot, mid, mid_hi, mid_lo, mid_lo2,
    h1_hi, h1_lo, h2_hi, h2_lo, t_hi, t_lo, gate_x,
    face, d_mix, out_nat,
    xi, gi, gi_y, di, di_y, mi, zi,
    acc_x, acc_y, acc_m, acc_o, acc_my, acc_oy,
    w_x, w_y, w_m, w_o, w_ot, w_mt, w_xt, w_yt,
):
    width = nat.shape[2]
    own = density.shape[2]
    blocks = own // 8
    ones = jnp.ones((16, width), BF16)
    fill_weights(
        (w_in, b_in, w_mid, b_mid, w_out, b_out), (w_x, w_y, w_m, w_o, w_ot, w_mt, w_xt, w_yt)
    )

    for c in range(4):
        if c == 0:
            source = density[0]
        elif c == 3:
            source = tracer[0]
        else:
            source = momentum[0, c - 1]
        nat[c, 8 : 8 + own, :] = source.T
        for side in range(2):
            edge = halo[side, 4 * c : 4 * c + 4, :]
            nat[c, 4 * side : 4 * side + 4, :] = edge
            nat[c, 8 + own + 4 * side : 12 + own + 4 * side, :] = edge
        put(cot, (c,), pl.ds(8, own), cotangent[0, c].T)
        for side in range(2):
            edge = halo[side, 16 + 4 * c : 20 + 4 * c, :]
            put(cot, (c,), pl.ds(4 * side, 4), edge)
            put(cot, (c,), pl.ds(8 + own + 4 * side, 4), edge)
    acc_x[...] = jnp.zeros_like(acc_x)
    acc_y[...] = jnp.zeros_like(acc_y)
    acc_m[...] = jnp.zeros_like(acc_m)
    acc_o[...] = jnp.zeros_like(acc_o)
    acc_my[...] = jnp.zeros_like(acc_my)
    acc_oy[...] = jnp.zeros_like(acc_oy)

    def middle(pre):
        firsts = [split3(jnp.tanh(v)) for v in pre]
        nexts = []
        for v in firsts:
            two = dot(w_m[...], rows(*v, v[0], ones))
            nexts.append(two[0:32] + two[32:64])
        return firsts, nexts

    def output(pre):
        seconds = [split3(jnp.tanh(v)) for v in pre]
        weight = w_o[...].astype(BF16)
        nexts = []
        for v in seconds:
            three = dot(weight, rows(*v, ones))
            nexts.append(three[0:8] + (three[8:16] + three[16:24]))
        return seconds, nexts

    def natural_gates(pre, gi):
        for line in range(8):
            put(gi, (), pl.ds(8 * line, 8), jnp.tanh(pre[line]))
        return [get(gi, (), pl.ds(g, 8, stride=8)) for g in range(8)]

    def back_output(gates, d_gates, di, load_second):
        for g in range(8):
            put(di, (), pl.ds(g, 8, stride=8), d_gates[g] * (1.0 - gates[g] * gates[g]))
        outs, pres = [], []
        for pair in range(4):
            o_hi, o_lo = split(get(di, (), pl.ds(16 * pair, 16)))
            outs.append((o_hi, o_lo))
            pres.append(dot(w_ot[...], rows(o_hi, o_lo, o_hi)))
        return outs, pres

    def back_through(pres, load, weight):
        parts, nexts = [], []
        for pair in range(4):
            s_hi, s_lo = load(pair)
            value = s_hi.astype(F32) + s_lo.astype(F32)
            part = split(pres[pair] * (1.0 - value * value))
            parts.append(part)
            if weight is not None:
                nexts.append(dot(weight[...], rows(part[0], part[1], part[0])))
        return parts, nexts

    def weight_sums(outs, d_second, load_first, load_second, acc_m, acc_o, valid):
        mid_lhs, mid_rhs, out_lhs, out_rhs = [], [], [], []
        for pair in range(4):
            f_hi, f_lo = load_first(pair)
            for line in range(2):
                at = slice(32 * line, 32 * line + 32)
                mid_lhs.append(rows(d_second[pair][0][at], d_second[pair][1][at]))
                mid_rhs.append(rows(f_hi[at], f_lo[at], ones))
            out_lhs.append(rows(*outs[pair]))
            out_rhs.append(rows(*load_second(pair), ones))
        acc_m[...] += jnp.where(valid, dot_nt(lanes(*mid_lhs), lanes(*mid_rhs)), 0.0)
        acc_o[...] += jnp.where(valid, dot_nt(lanes(*out_lhs), lanes(*out_rhs)), 0.0)

    def x_forward(b):
        n0 = pl.multiple_of(8 * b, 8)
        here = [nat[c, pl.ds(n0, 8), :] for c in range(4)]
        cells = [[roll(v, 1) for v in here], here, [roll(v, -1) for v in here], [roll(v, -2) for v in here]]
        for s in range(4):
            for c in range(4):
                put(xi, (), pl.ds(4 * s + c, 8, stride=16), cells[s][c])
        pre = []
        for line in range(8):
            window = split3(get(xi, (), pl.ds(16 * line, 16)))
            at = pl.ds(pl.multiple_of(128 * b + 16 * line, 16), 16)
            t_hi[at, :] = window[0]
            t_lo[at, :] = window[1]
            pre.append(dot(w_x[...], six(window, ones)))
        yield
        firsts, pre = middle(pre)
        for line in range(8):
            at = pl.ds(pl.multiple_of(256 * b + 32 * line, 32), 32)
            h1_hi[at, :] = firsts[line][0]
            h1_lo[at, :] = firsts[line][1]
        yield
        seconds, pre = output(pre)
        for line in range(8):
            at = pl.ds(pl.multiple_of(256 * b + 32 * line, 32), 32)
            h2_hi[at, :] = seconds[line][0]
            h2_lo[at, :] = seconds[line][1]
        yield
        gates = natural_gates(pre, gi)
        for g in range(8):
            gate_x[g, pl.ds(n0, 8), :] = gates[g]
        _, _, left, right = face_states(cells, gates)
        fluxes = flux_of(left, right)
        for c in range(4):
            value = here[c] - courant * (fluxes[c] - roll(fluxes[c], 1))
            put(mid, (c,), pl.ds(n0, 8), value)
            put(mi, (), pl.ds(Y_ORDER[c], 8, stride=4), value)
        at = pl.ds(pl.multiple_of(32 * b, 32), 32)
        for ref, part in zip((mid_hi, mid_lo, mid_lo2), split3(get(mi, (), pl.ds(0, 32)))):
            ref[at, :] = part
        yield

    d_mix[:, 0:16, :] = jnp.zeros((2, 16, 128), F32)

    def y_sweep(b, valid):
        n0 = pl.multiple_of(8 * b, 8)
        windows, pre = [], []
        for q in range(2):
            at = pl.ds(pl.multiple_of(32 * b + 16 * q, 16), 32)
            window = mid_hi[at, :], mid_lo[at, :], mid_lo2[at, :]
            windows.append(rows(window[0], window[1], ones))
            four = dot(w_y[...], six(window, ones))
            pre += [four[32 * line : 32 * line + 32] for line in range(4)]
        yield
        firsts, pre = middle(pre)
        yield
        seconds, pre = output(pre)
        yield
        gates = natural_gates(pre, gi_y)
        cells = [[get(mid, (c,), pl.ds(n0 + k, 8)) for c in Y_ORDER] for k in range(4)]
        cots = [courant * (get(cot, (c,), pl.ds(n0 + 2, 8)) - get(cot, (c,), pl.ds(n0 + 1, 8))) for c in Y_ORDER]
        d_gates, minus_below, to_here, to_above, minus_above2 = flux_back(cells, gates, cots)
        for c in range(4):
            to = Y_ORDER[c]
            put(face, (to,), pl.ds(n0, 8), minus_below[c])
            put(face, (4 + to,), pl.ds(n0, 8), to_here[c])
            put(face, (8 + to,), pl.ds(n0, 8), to_above[c])
            put(face, (12 + to,), pl.ds(n0, 8), minus_above2[c])

        def load(parts):
            return lambda pair: [rows(parts[2 * pair][k], parts[2 * pair + 1][k]) for k in range(2)]

        outs, pres = back_output(gates, d_gates, di_y, load(seconds))
        yield
        d_second, pres = back_through(pres, load(seconds), w_mt)
        yield
        d_first, _ = back_through(pres, load(firsts), None)
        combined, right_side = [], []
        for q in range(2):
            hi = rows(d_first[2 * q][0], d_first[2 * q + 1][0])
            lo = rows(d_first[2 * q][1], d_first[2 * q + 1][1])
            combined.append(dot(w_yt[...], rows(hi, lo, hi)))
            right_side.append(rows(hi, lo))
        yield
        weight_sums(outs, d_second, load(firsts), load(seconds), acc_my, acc_oy, valid)
        yield
        acc_y[...] += jnp.where(valid, dot_nt(lanes(*windows), lanes(*right_side)), 0.0)
        at = pl.multiple_of(32 * b, 32)
        put(d_mix, (), pl.ds(at, 16), get(d_mix, (), pl.ds(at, 16)) + combined[0][:16])
        put(d_mix, (), pl.ds(at + 16, 16), combined[0][16:] + combined[1][:16])
        put(d_mix, (), pl.ds(at + 32, 16), combined[1][16:])
        yield

    def x_back(b, valid):
        n0 = pl.multiple_of(8 * b, 8)
        gates = [gate_x[g, pl.ds(n0, 8), :] for g in range(8)]
        here = [nat[c, pl.ds(n0, 8), :] for c in range(4)]
        cells = [[roll(v, 1) for v in here], here, [roll(v, -1) for v in here], [roll(v, -2) for v in here]]
        back = []
        for c in range(4):
            value = get(cot, (c,), pl.ds(n0, 8)) + get(d_mix, (), pl.ds(4 * n0 + Y_ORDER[c], 8, stride=4))
            value = value + get(face, (4 + c,), pl.ds(n0 - 1, 8)) - get(face, (c,), pl.ds(n0, 8))
            value = value + get(face, (8 + c,), pl.ds(n0 - 2, 8)) - get(face, (12 + c,), pl.ds(n0 - 3, 8))
            back.append(value)
        cots = [courant * (roll(v, -1) - v) for v in back]
        d_gates, minus_below, to_here, to_above, minus_above2 = flux_back(cells, gates, cots)

        def load(hi_ref, lo_ref):
            def of(pair):
                at = pl.ds(pl.multiple_of(256 * b + 64 * pair, 64), 64)
                return hi_ref[at, :], lo_ref[at, :]
            return of

        first, second = load(h1_hi, h1_lo), load(h2_hi, h2_lo)
        outs, pres = back_output(gates, d_gates, di, second)
        direct = [
            (back[c] + to_here[c], minus_below[c], to_above[c], minus_above2[c]) for c in range(4)
        ]
        yield
        d_second, pres = back_through(pres, second, w_mt)
        yield
        d_first, _ = back_through(pres, first, None)
        left_side, right_side = [], []
        for line in range(8):
            at = pl.ds(pl.multiple_of(128 * b + 16 * line, 16), 16)
            left_side.append(rows(t_hi[at, :], t_lo[at, :], ones))
            at = slice(32 * (line % 2), 32 * (line % 2) + 32)
            hi, lo = [v[at] for v in d_first[line // 2]]
            right_side.append(rows(hi, lo))
            put(zi, (), pl.ds(16 * line, 16), dot(w_xt[...], rows(hi, lo, hi)))
        yield
        weight_sums(outs, d_second, first, second, acc_m, acc_o, valid)
        acc_x[...] += jnp.where(valid, dot_nt(lanes(*left_side), lanes(*right_side)), 0.0)
        yield
        for c in range(4):
            parts = [get(zi, (), pl.ds(4 * s + c, 8, stride=16)) for s in range(4)]
            value = direct[c][0] + parts[1] + roll(parts[0] - direct[c][1], -1)
            value = value + roll(direct[c][2] + parts[2], 1) + roll(parts[3] - direct[c][3], 2)
            out_nat[c, pl.ds(pl.multiple_of(n0 - 8, 8), 8), :] = value
        yield

    def step(i, carry):
        back = x_back(jnp.maximum(i - 3, 1), i >= 4)
        sweep = y_sweep(jnp.maximum(i - 2, 0), jnp.logical_and(i >= 3, i <= blocks + 2))
        ahead = x_forward(i)
        for stage in STAGES:
            next({"b": back, "y": sweep, "f": ahead}[stage])
        return carry

    lax.fori_loop(0, blocks + 4, step, 0)

    g_density[0] = out_nat[0].T
    g_momentum[0, 0] = out_nat[1].T
    g_momentum[0, 1] = out_nat[2].T
    g_tracer[0] = out_nat[3].T

    acc_m[...] += acc_my[...]
    acc_o[...] += acc_oy[...]
    r, k = index((24, 48), 0), index((24, 48), 1)
    pick = jnp.where(k < 32, k % 16, jnp.where(k == 32, 16, -1))
    first_x = exact(indicator(r == pick), acc_x[...])
    r, k = index((80, 256), 0), index((80, 256), 1)
    distance = (r // 4) % 8 - (k // 32) % 4
    rr, kk = index((24, 80), 0), index((24, 80), 1)
    masked = jnp.where(r == 64, acc_y[...], 0.0)
    first_y = exact(indicator(jnp.logical_and(rr == 16, kk == 64)), masked)
    for s in range(4):
        masked = jnp.where(jnp.logical_and(r < 64, distance == s), acc_y[...], 0.0)
        first_y = first_y + exact(indicator(jnp.logical_and(rr == 4 * s + kk % 4, kk < 64)), masked)

    def by_unit(shape, axis):
        return indicator(index(shape, axis) % 32 == index(shape, 1 - axis))

    first = exact(by_unit((32, 64), 1), first_x, nt=True) + exact(by_unit((32, 256), 1), first_y, nt=True)
    first_bias = exact(first_x, by_unit((64, 32), 0)) + exact(first_y, by_unit((256, 32), 0))
    r, k = index((24, 128), 0), index((24, 128), 1)
    total = exact(first, indicator(jnp.logical_and(k == r + 64, r < 16)))
    r, k = index((80, 128), 0), index((80, 128), 1)
    total = total + exact(exact(by_unit((32, 64), 1), acc_m[...]), indicator(jnp.logical_and(r % 32 == k, r < 64)))
    second_bias = exact(exact(indicator(index((8, 80), 1) == 64), acc_m[...], nt=True), by_unit((64, 32), 0))
    r, k = index((32, 144), 0), index((32, 144), 1)
    masked = jnp.where(jnp.logical_and(k < 128, (r // 8) % 2 == (k // 32) % 2), acc_o[...], 0.0)
    r, k = index((8, 32), 0), index((8, 32), 1)
    summed = exact(indicator(r == k % 8), masked)
    r, k = index((144, 128), 0), index((144, 128), 1)
    packed[0:8, :] = total[0:8] + exact(summed, indicator(jnp.logical_and(r % 32 + 96 == k, r < 128)))
    packed[16:32, :] = total[16:32]
    out_bias = exact(indicator(index((8, 144), 1) == 128), acc_o[...], nt=True)
    r, k = index((32, 128), 0), index((32, 128), 1)
    out_bias = exact(out_bias, indicator(r % 8 + 96 == k))
    r, k = index((32, 128), 0), index((32, 128), 1)
    wide = indicator(r + 96 == k)
    first_bias = exact(first_bias[16:24], wide)
    second_bias = exact(second_bias, wide)
    r = index((8, 128), 0)
    first_bias = jnp.broadcast_to(first_bias[0:1], (8, 128))
    packed[8:16, :] = total[8:16] + jnp.where(
        r == 0, first_bias, jnp.where(r == 1, second_bias, jnp.where(r == 2, out_bias, 0.0))
    )


def halo_kernel(size, inner, density, momentum, tracer, cotangent, halo, sent, landed, send_sem, recv_sem):
    mesh_ids = pl.DeviceIdType.MESH
    here = lax.axis_index("tx") * inner + lax.axis_index("ty")
    peers = []
    for step in (size - 1, 1):
        peer = lax.rem(here + step, size)
        peers.append({"tx": peer // inner, "ty": lax.rem(peer, inner)})
    barrier = pltpu.get_barrier_semaphore()
    for peer in peers:
        pl.semaphore_signal(barrier, inc=1, device_id=peer, device_id_type=mesh_ids)
    own = density.shape[2]
    for c in range(8):
        if c >= 4:
            source = cotangent[0, c - 4]
        elif c == 0:
            source = density[0]
        elif c == 3:
            source = tracer[0]
        else:
            source = momentum[0, c - 1]
        lines = source.T
        sent[0, 4 * c : 4 * c + 4, :] = lines[:HALO]
        sent[1, 4 * c : 4 * c + 4, :] = lines[own - HALO :]
    pl.semaphore_wait(barrier, 2)
    copies = [
        pltpu.make_async_remote_copy(
            src_ref=sent.at[side],
            dst_ref=landed.at[side],
            send_sem=send_sem.at[side],
            recv_sem=recv_sem.at[side],
            device_id=peers[side],
            device_id_type=mesh_ids,
        )
        for side in range(2)
    ]
    for copy in copies:
        copy.start()
    for copy in copies:
        copy.wait()
    halo[...] = landed[...]


GROUPS = ("traj", "ty", "tx")


def reduce_kernel(sizes, mine, total, *scratch):
    count = len(sizes)
    slots, sends, receives = scratch[:count], scratch[count : 2 * count], scratch[2 * count :]
    mesh_ids = pl.DeviceIdType.MESH
    barrier = pltpu.get_barrier_semaphore()
    for axis, size in zip(GROUPS, sizes):
        here = lax.axis_index(axis)
        for step in range(1, size):
            peer = lax.rem(here + step, size)
            pl.semaphore_signal(barrier, inc=1, device_id={axis: peer}, device_id_type=mesh_ids)
    pl.semaphore_wait(barrier, sum(sizes) - count)
    value = mine[...]
    for at, (axis, size) in enumerate(zip(GROUPS, sizes)):
        here = lax.axis_index(axis)
        slots[at][here] = value
        copies = []
        for step in range(1, size):
            peer = lax.rem(here + step, size)
            copies.append(
                pltpu.make_async_remote_copy(
                    src_ref=slots[at].at[here],
                    dst_ref=slots[at].at[here],
                    send_sem=sends[at].at[step],
                    recv_sem=receives[at].at[step],
                    device_id={axis: peer},
                    device_id_type=mesh_ids,
                )
            )
        for copy in copies:
            copy.start()
        for copy in copies:
            copy.wait()
        value = slots[at][0]
        for other in range(1, size):
            value = value + slots[at][other]
    total[...] = value


def unpack_kernel(total, g_w_in, g_b_in, g_w_mid, g_b_mid, g_w_out, g_b_out):
    g_w_in[...] = total[0:32, :].T[64:80]
    g_b_in[...] = total[8:9, 96:128]
    g_w_mid[...] = total[0:32, 0:32]
    g_b_mid[...] = total[9:10, 96:128]
    g_w_out[...] = total[0:8, 96:128]
    g_b_out[...] = total[10:11, 96:104]


def ring_size(mesh):
    return mesh.shape["tx"] * mesh.shape["ty"]


def make_body(size, inner, sizes):
    def body(density, momentum, tracer, cotangent, w_in, b_in, w_mid, b_mid, w_out, b_out):
        own, width = density.shape[2], density.shape[1]
        in_vmem = pl.BlockSpec(memory_space=pltpu.VMEM)
        halo_shape = (2, 8 * HALO, width)
        halo = pl.pallas_call(
            functools.partial(halo_kernel, size, inner),
            out_shape=jax.ShapeDtypeStruct(halo_shape, F32),
            in_specs=[in_vmem] * 4,
            out_specs=in_vmem,
            scratch_shapes=[pltpu.VMEM(halo_shape, F32)] * 2 + [pltpu.SemaphoreType.DMA((2,))] * 2,
            compiler_params=pltpu.CompilerParams(collective_id=1, has_side_effects=True),
        )(density, momentum, tracer, cotangent)
        biases = [b.reshape(1, -1) for b in (b_in, b_mid, b_out)]
        weights = (w_in.T, biases[0], w_mid, biases[1], w_out, biases[2])
        extra = own + 32
        lines = own + 32
        out = pl.pallas_call(
            kernel,
            out_shape=(
                jax.ShapeDtypeStruct(density.shape, F32),
                jax.ShapeDtypeStruct(momentum.shape, F32),
                jax.ShapeDtypeStruct(tracer.shape, F32),
                jax.ShapeDtypeStruct((32, 128), F32),
            ),
            in_specs=[pl.BlockSpec(memory_space=pltpu.VMEM)] * 11,
            out_specs=tuple([pl.BlockSpec(memory_space=pltpu.VMEM)] * 4),
            scratch_shapes=[
                pltpu.VMEM((4, lines, width), F32),
                pltpu.VMEM((4, 2, extra, 128), F32),
                pltpu.VMEM((4, 2, extra, 128), F32),
                pltpu.VMEM((4 * extra, width), BF16),
                pltpu.VMEM((4 * extra, width), BF16),
                pltpu.VMEM((4 * extra, width), BF16),
                pltpu.VMEM((32 * lines, width), BF16),
                pltpu.VMEM((32 * lines, width), BF16),
                pltpu.VMEM((32 * lines, width), BF16),
                pltpu.VMEM((32 * lines, width), BF16),
                pltpu.VMEM((16 * lines, width), BF16),
                pltpu.VMEM((16 * lines, width), BF16),
                pltpu.VMEM((8, lines, width), F32),
                pltpu.VMEM((16, 2, extra, 128), F32),
                pltpu.VMEM((2, 4 * extra, 128), F32),
                pltpu.VMEM((4, own, width), F32),
                pltpu.VMEM((2, 128, 128), F32),
                pltpu.VMEM((2, 64, 128), F32),
                pltpu.VMEM((2, 64, 128), F32),
                pltpu.VMEM((2, 64, 128), F32),
                pltpu.VMEM((2, 64, 128), F32),
                pltpu.VMEM((2, 32, 128), F32),
                pltpu.VMEM((2, 128, 128), F32),
                pltpu.VMEM((48, 64), F32),
                pltpu.VMEM((80, 256), F32),
                pltpu.VMEM((64, 80), F32),
                pltpu.VMEM((32, 144), F32),
                pltpu.VMEM((64, 80), F32),
                pltpu.VMEM((32, 144), F32),
                pltpu.VMEM((32, 112), BF16),
                pltpu.VMEM((128, 208), BF16),
                pltpu.VMEM((64, 144), BF16),
                pltpu.VMEM((24, 112), F32),
                pltpu.VMEM((64, 48), BF16),
                pltpu.VMEM((64, 192), BF16),
                pltpu.VMEM((16, 96), BF16),
                pltpu.VMEM((32, 384), BF16),
            ],
            compiler_params=pltpu.CompilerParams(vmem_limit_bytes=60 * 1024 * 1024),
        )(density, momentum, tracer, cotangent, halo, *weights)
        shape = (32, 128)
        total = pl.pallas_call(
            functools.partial(reduce_kernel, sizes),
            out_shape=jax.ShapeDtypeStruct(shape, F32),
            in_specs=[in_vmem],
            out_specs=in_vmem,
            scratch_shapes=[pltpu.VMEM((n,) + shape, F32) for n in sizes]
            + [pltpu.SemaphoreType.DMA((n,)) for n in sizes] * 2,
            compiler_params=pltpu.CompilerParams(collective_id=0, has_side_effects=True),
        )(out[3])
        totals = pl.pallas_call(
            unpack_kernel,
            out_shape=tuple(jax.ShapeDtypeStruct(w.shape, F32) for w in weights),
            in_specs=[in_vmem],
            out_specs=tuple([in_vmem] * 6),
        )(total)
        return (
            out[0],
            out[1],
            out[2],
            totals[0].T,
            totals[1].reshape(-1),
            totals[2],
            totals[3].reshape(-1),
            totals[4],
            totals[5].reshape(-1),
        )

    return body


def solution(mesh):
    in_specs = (
        P("traj", None, ("tx", "ty")),
        P("traj", None, None, ("tx", "ty")),
        P("traj", None, ("tx", "ty")),
        P("traj", None, None, ("tx", "ty")),
        P(), P(), P(), P(), P(), P(),
    )
    out_specs = (
        P("traj", None, ("tx", "ty")),
        P("traj", None, None, ("tx", "ty")),
        P("traj", None, ("tx", "ty")),
        P(), P(), P(), P(), P(), P(),
    )
    return jax.shard_map(
        make_body(ring_size(mesh), mesh.shape["ty"], tuple(mesh.shape[axis] for axis in GROUPS)), mesh=mesh, in_specs=in_specs, out_specs=out_specs, check_vma=False
    )
```
